512 devices in a mesh: var: 32 (over x, y), tp: 16 (over z, core).
Axes of the slice: x: 4, y: 8, z: 8, core: 2. Of those that a mesh axis runs over, the one named last changes fastest.
Arguments:
- projected: bfloat16 [1024, 32, 3, 8192], P(('var', 'tp')), may hold values from -6 to 6
- cache_history: bfloat16 [192, 127, 8192], P('var', None, 'tp'), may hold values from -6 to 6
- cache_inputs: bfloat16 [192, 6, 3, 8192], P('var', None, None, 'tp'), may hold values from -6 to 6
- feature_taps: bfloat16 [7, 3, 8192], P(None, None, 'tp'), may hold values from -2 to 2
- filters: bfloat16 [128, 512], P(None, 'tp'), may hold values from -0.5 to 0.5
- skip_weight: bfloat16 [8192], P('tp'), may hold values from -4 to 4
- base_inputs: bfloat16 [4, 3, 8192], P(None, None, 'tp'), may hold values from -6 to 6
- window_owner: int32 [1024, 1], replicated, may hold values from 0 to 31; in each aligned block of 32 rows (0 to 31, 32 to 63, ...) at most 2 rows name the same one
- window_slot: int32 [1024], replicated, may hold values from 0 to 5
- variant_position: int32 [1024], P('var'), may hold values from 0 to 31
- allele: int32 [1024], P('var'), may hold values from 0 to 3
Outputs:
- mixer_out: bfloat16 [1024, 32, 8192], P(('var', 'tp'))
The draws below stay inside these ranges and needn't reach their ends.
Inputs may be any that keep to these rules, and one draw needn't show every extreme that they name: `window_owner`: among the windows of one index of var (aligned blocks of 32 rows), at most 2 name the same owner.
All inputs are finite; a program needn't handle non-finite values.
Results may differ from the reference program's by a relative error of at most 0.0049.
Values may be sent and summed in bfloat16 or wider, within the bound.
No kernel may reach another device: no remote copies, remote signals or barrier semaphores. Data moves between devices by JAX's collectives and lax.ppermute only.
A program may use at most 128 MiB of HBM per device.

```python
import math
import jax
import jax.numpy as jnp
import numpy as np
from jax import lax

D = 8192
FGROUP = 16
FEAT_TAPS = 7
FILT_TAPS = 128
BASES = 4
WLEN = 32
SLOTS = 6
WIN_DEV = 32
CAP = 2
WINDOWS = 1024
LOCI = 192
OWNERS = 32
N_VAR = 32


def with_ends(entries, key, low, high):
    place = [jax.random.randint(jax.random.fold_in(key, axis), (), 0, length) for axis, length in enumerate(entries.shape)]
    widest = entries.shape.index(max(entries.shape))
    beside = place[:widest] + [(place[widest] + 1) % entries.shape[widest]] + place[widest + 1:]
    return entries.at[tuple(place)].set(low).at[tuple(beside)].set(high)


def levels(key, dims, cuts, least, top_value):
    def one(dim, shards_of):
        draws = jax.random.uniform(jax.random.fold_in(jax.random.fold_in(key, 6), dim), (shards_of,), jnp.float32, least / len(cuts), top_value / len(cuts))
        return jnp.repeat(jnp.exp(draws), dims[dim] // shards_of).reshape((-1,) + (1,) * (len(dims) - dim - 1))

    gain = one(*cuts[0])
    for cut in cuts[1:]:
        gain = gain * one(*cut)
    return gain


def deal_out(own_key, own, number, rows, number_of, top, bound, skew):
    sequence = jax.random.permutation(own_key, number_of)
    packed, common = shares(number_of, rows * top, bound, skew, True), shares(number_of, rows * top, bound, skew, False)
    places = jnp.arange(number_of)

    def named(lengths, offset_by):
        used = int((lengths > 0).sum())
        fixed = max(1, used // 4)
        passed = fixed + (places - fixed + offset_by * (used - fixed)) % max(1, number_of - fixed)
        return jnp.zeros((number_of,), jnp.int32).at[sequence[jnp.where(places < fixed, places, passed)]].set(jnp.asarray(lengths, jnp.int32))

    lengths = jnp.where(number % 4 == 0, named(packed, number // 4), named(common, number - number // 4 - 1))
    mixed = jax.random.permutation(jax.random.fold_in(own, 3), number_of)
    donor, taker = mixed[0:number_of // 2 * 2:2], mixed[1:number_of // 2 * 2:2]
    room = jnp.minimum(lengths[donor] - 1, bound - lengths[taker]) // 2
    room = jnp.where((donor == sequence[0]) | (taker == sequence[0]) | (lengths[taker] == 0), 0, jnp.maximum(room, 0))
    passed = jax.random.randint(jax.random.fold_in(own, 4), (number_of // 2,), 0, 1 << 20) % (room + 1)
    lengths = lengths.at[donor].add(-passed).at[taker].add(passed)
    members = jnp.searchsorted(jnp.cumsum(lengths), jnp.arange(rows * top), side="right").astype(jnp.int32)
    listing = members.reshape(top, rows).T
    listing = listing[jax.random.permutation(jax.random.fold_in(own, 1), rows)]
    offset_by = jax.random.randint(jax.random.fold_in(own, 2), (rows, 1), 0, top)
    return jnp.take_along_axis(listing, (jnp.arange(top)[None, :] + offset_by) % top, axis=1)


def shares(number_of, total, reach, skew, full):
    loads = [(1 << 20) // math.isqrt(rank ** skew) + 1 for rank in range(1, number_of + 1)]
    largest = reach if full else min(reach, max(-(-total // number_of), total * loads[0] // sum(loads)))
    least = 1 if total - largest >= number_of - 1 else 0
    counts, surplus = [largest] + [least] * (number_of - 1), total - largest - least * (number_of - 1)
    while surplus > 0:
        free = [i for i in range(1, number_of) if counts[i] < largest] or [i for i in range(1, number_of) if counts[i] < reach]
        whole, left = sum([loads[i] for i in free]), surplus
        for i in free:
            extra = min(reach - counts[i], max(1, left * loads[i] // whole), surplus)
            counts[i] = counts[i] + extra
            surplus = surplus - extra
    return np.array(counts)


def scatter_about(rng, extent, spread, limit, split=(), dtype=jnp.bfloat16):
    array = spread * jax.random.normal(rng, extent, jnp.float32)
    if split:
        array = array * levels(rng, extent, split, -0.22, 0.18)
    return jnp.clip(array, -limit, limit).astype(dtype)


def setup_inputs(seed: int = 0) -> dict:
    key_of = jax.random.split(jax.random.key(seed), 12)
    projected = scatter_about(key_of[0], (WINDOWS, WLEN, 3, D), 1.0, 6.0, ((0, 512),))
    cache_history = scatter_about(key_of[1], (LOCI, FILT_TAPS - 1, D), 1.0, 6.0, ((0, 32), (2, 16)))
    cache_inputs = scatter_about(key_of[2], (LOCI, FEAT_TAPS - 1, 3, D), 1.0, 6.0, ((0, 32), (3, 16)))
    feature_taps = scatter_about(key_of[3], (FEAT_TAPS, 3, D), FEAT_TAPS ** -0.5, 2.0, ((2, 16),))
    filters = scatter_about(key_of[4], (FILT_TAPS, D // FGROUP), FILT_TAPS ** -0.5, 0.5, ((1, 16),))
    skip_weight = scatter_about(key_of[5], (D,), 1.0, 4.0, ((0, 16),))
    base_inputs = scatter_about(key_of[6], (BASES, 3, D), 1.0, 6.0, ((2, 16),))
    window_owner_keys = jax.random.split(jax.random.fold_in(key_of[7], 1), WINDOWS // WIN_DEV)
    window_owner_turns = jax.random.permutation(jax.random.fold_in(key_of[7], 3), WINDOWS // WIN_DEV)
    window_owner = jax.vmap(lambda own, number: deal_out(jax.random.fold_in(key_of[7], 2), own, number, WIN_DEV, OWNERS, 1, CAP, 2))(window_owner_keys, window_owner_turns).reshape((WINDOWS, 1))
    window_slot = with_ends(jax.random.randint(key_of[8], (WINDOWS,), 0, SLOTS), jax.random.fold_in(key_of[8], 1), 0, SLOTS - 1).astype(jnp.int32)
    variant_position = with_ends(jax.random.randint(key_of[9], (WINDOWS,), 0, WLEN), jax.random.fold_in(key_of[9], 1), 0, WLEN - 1).astype(jnp.int32)
    allele = with_ends(jax.random.randint(key_of[10], (WINDOWS,), 0, BASES), jax.random.fold_in(key_of[10], 1), 0, BASES - 1).astype(jnp.int32)
    return dict(projected=projected, cache_history=cache_history, cache_inputs=cache_inputs, feature_taps=feature_taps, filters=filters, skip_weight=skip_weight, base_inputs=base_inputs, window_owner=window_owner, window_slot=window_slot, variant_position=variant_position, allele=allele)


def tap_table(filters, row_count, col_count, offset):
    tap_count = filters.shape[0]
    lag_index = jnp.arange(row_count)[:, None] + offset - jnp.arange(col_count)[None, :]
    inside_range = (lag_index >= 0) & (lag_index < tap_count)
    picked = jnp.take(filters.astype(jnp.float32), jnp.clip(lag_index, 0, tap_count - 1), axis=0)
    return jnp.where(inside_range[:, :, None], picked, jnp.float32(0.0))


def grouped_filter(table, values):
    item_count, length, channel_count = values.shape
    groups = table.shape[2]
    shaped = values.reshape(item_count, length, groups, channel_count // groups)
    result = jnp.einsum("tsg,nsgc->ntgc", table, shaped)
    return result.reshape(item_count, table.shape[0], channel_count)


def reference(projected, cache_history, cache_inputs, feature_taps, filters, skip_weight, base_inputs, window_owner, window_slot, variant_position, allele):
    window_count = projected.shape[0]
    window_len = projected.shape[1]
    history_len = cache_history.shape[1]
    lead_len = cache_inputs.shape[1]
    locus = (window_owner[:, 0] * SLOTS + window_slot).astype(jnp.int32)
    table_win = tap_table(filters, window_len, window_len, 0)
    table_pre = tap_table(filters, window_len, history_len, history_len)

    def one_block(pieces):
        input_block, locus_block, position_block, allele_block = pieces
        base_rows = jnp.take(base_inputs, allele_block, axis=0)
        placed = jnp.arange(window_len)[None, :] == position_block[:, None]
        altered = jnp.where(placed[:, :, None, None], base_rows[:, None], input_block)
        extended = jnp.concatenate([jnp.take(cache_inputs, locus_block, axis=0), altered], axis=1)
        featured = jnp.zeros(altered.shape, jnp.float32)
        for tap_index in range(FEAT_TAPS):
            start_row = lead_len - tap_index
            featured = featured + feature_taps[tap_index].astype(jnp.float32) * extended[:, start_row:start_row + window_len].astype(jnp.float32)
        mixed_in = lax.optimization_barrier((featured[:, :, 1] * featured[:, :, 2]).astype(jnp.bfloat16)).astype(jnp.float32)
        inside = grouped_filter(table_win, mixed_in)
        history = jnp.take(cache_history, locus_block, axis=0).astype(jnp.float32)
        carried = lax.optimization_barrier(grouped_filter(table_pre, history).astype(jnp.bfloat16)).astype(jnp.float32)
        filtered = inside + carried + skip_weight.astype(jnp.float32) * mixed_in
        return (featured[:, :, 0] * filtered).astype(jnp.bfloat16)

    pieces = (projected.reshape((N_VAR, WIN_DEV) + projected.shape[1:]), locus.reshape(N_VAR, WIN_DEV), variant_position.reshape(N_VAR, WIN_DEV), allele.reshape(N_VAR, WIN_DEV))
    mixed_all = lax.map(one_block, pieces)
    return mixed_all.reshape(window_count, window_len, projected.shape[3])
```

```python
import functools
import jax
import jax.numpy as jnp
from jax import lax
from jax.experimental import pallas as pl
from jax.experimental.pallas import tpu as pltpu
from jax.sharding import PartitionSpec as P

LANES = 128
TAP_ROWS = 40
TIME = 32


def owner_kernel(group_size, history_ref, inputs_ref, filters_ref, taps_ref, base_ref, skip_ref,
                 lead_ref, carried_ref, param_ref, line_scr, lead_scr, param_scr):
    loci, history_len, width = history_ref.shape
    lead_len, streams = inputs_ref.shape[1:3]
    taps, bases = taps_ref.shape[1], base_ref.shape[1]
    groups, tap_count = filters_ref.shape
    blocks = width // LANES
    per_block = LANES // group_size
    f32 = jnp.float32
    for n in range(loci):
        for r in range(lead_len):
            for b in range(blocks):
                at = ((n * blocks + b) * lead_len + r) * streams
                piece = inputs_ref[n, r, :, b * LANES : (b + 1) * LANES]
                lead_scr[at : at + streams, :] = piece.astype(f32)
    span = blocks * lead_len * streams
    for n in range(loci):
        lead_ref[n] = lead_scr[n * span : (n + 1) * span, :].astype(jnp.bfloat16)
    param_scr[...] = jnp.zeros_like(param_scr)
    for s in range(streams):
        param_scr[s * taps : (s + 1) * taps, :] = taps_ref[s].astype(f32)
        at = streams * taps + s * bases
        param_scr[at : at + bases, :] = base_ref[s].astype(f32)
    at = streams * (taps + bases)
    param_scr[at : at + 1, :] = skip_ref[...].astype(f32)
    owner = lax.broadcasted_iota(jnp.int32, (groups, width), 1) // group_size
    spread = (owner == lax.broadcasted_iota(jnp.int32, (groups, width), 0)).astype(jnp.bfloat16)
    wide = lax.dot_general(
        filters_ref[...], spread, (((0,), (0,)), ((), ())), preferred_element_type=f32
    )
    param_ref[:TAP_ROWS, :] = param_scr[...].astype(jnp.bfloat16)
    param_ref[TAP_ROWS:, :] = wide[:TIME].astype(jnp.bfloat16)

    row = lax.broadcasted_iota(jnp.int32, (tap_count, tap_count), 0)
    col = lax.broadcasted_iota(jnp.int32, (tap_count, tap_count), 1)
    flip = (row + col == tap_count - 1).astype(jnp.bfloat16)
    line_scr[...] = jnp.dot(filters_ref[...], flip, preferred_element_type=f32)
    t_row = lax.broadcasted_iota(jnp.int32, (TIME, tap_count), 0)
    s_col = lax.broadcasted_iota(jnp.int32, (TIME, tap_count), 1)
    valid = (s_col >= t_row) & (s_col < history_len)
    lane = lax.broadcasted_iota(jnp.int32, (TIME, LANES), 1) // group_size
    for b in range(blocks):
        tables = []
        for g in range(per_block):
            index = b * per_block + g
            line = jnp.broadcast_to(line_scr[index : index + 1, :], (TIME, tap_count))
            turned = pltpu.roll(line, 0, 1, stride=1, stride_axis=0)
            tables.append(jnp.where(valid, turned, 0.0))
        table = jnp.concatenate(tables, axis=0).astype(jnp.bfloat16)[:, :history_len]
        for n in range(loci):
            past = history_ref[n, :, b * LANES : (b + 1) * LANES]
            full = jnp.dot(table, past, preferred_element_type=f32)
            total = jnp.zeros((TIME, LANES), f32)
            for g in range(per_block):
                total = jnp.where(lane == g, full[g * TIME : (g + 1) * TIME], total)
            carried_ref[n, b * TIME : (b + 1) * TIME, :] = total.astype(jnp.bfloat16)


def owner_of(history, inputs, filters_t, taps, base, skip, group_size):
    loci, _, width = history.shape
    lead_len, streams = inputs.shape[1:3]
    blocks = width // LANES
    shape = lambda *dims: jax.ShapeDtypeStruct(dims, jnp.bfloat16)
    return pl.pallas_call(
        functools.partial(owner_kernel, group_size),
        out_shape=(
            shape(loci, blocks * lead_len * streams, LANES),
            shape(loci, blocks * TIME, LANES),
            shape(TAP_ROWS + TIME, width),
        ),
        in_specs=[pl.BlockSpec(memory_space=pltpu.VMEM)] * 6,
        out_specs=[pl.BlockSpec(memory_space=pltpu.VMEM)] * 3,
        scratch_shapes=[
            pltpu.VMEM(filters_t.shape, jnp.float32),
            pltpu.VMEM((loci * blocks * lead_len * streams, LANES), jnp.float32),
            pltpu.VMEM((TAP_ROWS, width), jnp.float32),
        ],
        name="owner",
    )(history, inputs, filters_t, taps, base, skip)


def mixer_kernel(dims, pos_ref, allele_ref, proj_ref, lead_ref, carried_ref, param_ref,
                 out_ref, x_scr, l_scr, c_scr, p_scr, f_scr, m_scr, o_scr):
    taps, bases, streams, lead_len = dims
    wins, _, _, width = proj_ref.shape
    blocks = width // LANES
    rows = wins * blocks
    lead_rows = lead_len * streams
    f32 = jnp.float32
    for w in range(wins):
        for b in range(blocks):
            q = w * blocks + b
            lanes = slice(b * LANES, (b + 1) * LANES)
            p_scr[q * TAP_ROWS : (q + 1) * TAP_ROWS, :] = param_ref[0, :TAP_ROWS, lanes].astype(f32)
            f_scr[q * TIME : (q + 1) * TIME, :] = param_ref[0, TAP_ROWS:, lanes].astype(f32)
            for s in range(streams):
                x_scr[s, q * TIME : (q + 1) * TIME, :] = proj_ref[w, s, :, lanes].astype(f32)
        span = blocks * lead_rows
        l_scr[w * span : (w + 1) * span, :] = lead_ref[0, w].astype(f32)
        span = blocks * TIME
        c_scr[w * span : (w + 1) * span, :] = carried_ref[0, w].astype(f32)
    for w in range(wins):
        for s in range(streams):
            for b in range(blocks):
                q = w * blocks + b
                source = q * TAP_ROWS + streams * taps + s * bases + allele_ref[w]
                x_scr[s, pl.ds(q * TIME + pos_ref[w], 1), :] = p_scr[pl.ds(source, 1), :]

    def param(r):
        return p_scr[pl.ds(r, rows, stride=TAP_ROWS), :]

    def entry(s, r):
        if r < lead_len:
            return l_scr[pl.ds(r * streams + s, rows, stride=lead_rows), :]
        return x_scr[s, pl.ds(r - lead_len, rows, stride=TIME), :]

    def featured(s):
        weight = [param(s * taps + j) for j in range(taps)]
        window = [entry(s, r) for r in range(taps - 1)]
        for t in range(TIME):
            window.append(entry(s, t + taps - 1))
            total = weight[0] * window[taps - 1]
            for j in range(1, taps):
                total = total + weight[j] * window[taps - 1 - j]
            window.pop(0)
            yield total

    for t, (one, two) in enumerate(zip(featured(1), featured(2))):
        m_scr[t] = (one * two).astype(jnp.bfloat16).astype(f32)
    skip = param(streams * (taps + bases))
    gates = featured(0)
    step = 8
    for start in range(0, TIME, step):
        total = [None] * step
        for j in range(start + step):
            tap = f_scr[pl.ds(j, rows, stride=TIME), :]
            for i in range(step):
                at = start + i - j
                if at >= 0:
                    term = tap * m_scr[at]
                    total[i] = term if total[i] is None else total[i] + term
        for i in range(step):
            t = start + i
            carried = c_scr[pl.ds(t, rows, stride=TIME), :]
            filtered = total[i] + carried + skip * m_scr[t]
            o_scr[pl.ds(t, rows, stride=TIME), :] = next(gates) * filtered
    for w in range(wins):
        for b in range(blocks):
            q = w * blocks + b
            lanes = slice(b * LANES, (b + 1) * LANES)
            out_ref[w, :, lanes] = o_scr[q * TIME : (q + 1) * TIME, :].astype(jnp.bfloat16)


def mixer_of(dims, position, allele, proj, lead, carried, params):
    taps, bases, streams, lead_len = dims
    wins, _, _, total = proj.shape
    parts = params.shape[0]
    width = total // parts
    blocks = width // LANES
    rows = wins * blocks
    spec = pltpu.PrefetchScalarGridSpec(
        num_scalar_prefetch=2,
        grid=(parts,),
        in_specs=[
            pl.BlockSpec((wins, streams, TIME, width), lambda k, *_: (0, 0, 0, k)),
            pl.BlockSpec((1, wins, blocks * lead_len * streams, LANES), lambda k, *_: (k, 0, 0, 0)),
            pl.BlockSpec((1, wins, blocks * TIME, LANES), lambda k, *_: (k, 0, 0, 0)),
            pl.BlockSpec((1, TAP_ROWS + TIME, width), lambda k, *_: (k, 0, 0)),
        ],
        out_specs=pl.BlockSpec((wins, TIME, width), lambda k, *_: (0, 0, k)),
        scratch_shapes=[
            pltpu.VMEM((streams, rows * TIME, LANES), jnp.float32),
            pltpu.VMEM((rows * lead_len * streams, LANES), jnp.float32),
            pltpu.VMEM((rows * TIME, LANES), jnp.float32),
            pltpu.VMEM((rows * TAP_ROWS, LANES), jnp.float32),
            pltpu.VMEM((rows * TIME, LANES), jnp.float32),
            pltpu.VMEM((TIME, rows, LANES), jnp.float32),
            pltpu.VMEM((rows * TIME, LANES), jnp.float32),
        ],
    )
    return pl.pallas_call(
        functools.partial(mixer_kernel, dims),
        out_shape=jax.ShapeDtypeStruct((wins, TIME, total), jnp.bfloat16),
        grid_spec=spec,
        name="mixer",
    )(position, allele, proj, lead, carried, params)

def exchange(packed, window_owner, window_slot, me, windows):
    var_count = lax.axis_size("var")
    capacity = 2
    owners = window_owner[:, 0].reshape(var_count, windows)
    slots = window_slot.reshape(var_count, windows)
    mine = owners == me
    rank = jnp.cumsum(mine.astype(jnp.int32), axis=1) - 1
    hit = mine[:, None, :] & (rank[:, None, :] == jnp.arange(capacity)[None, :, None])
    pick = jnp.sum(jnp.where(hit, slots[:, None, :], 0), axis=2).reshape(-1)
    send = packed.at[pick].get(mode="promise_in_bounds")
    send = send.reshape(var_count, capacity * packed.shape[1], LANES)
    got = lax.all_to_all(send, "var", split_axis=0, concat_axis=0, tiled=True)
    got = got.reshape(var_count * capacity, packed.shape[1], LANES)
    own_owner = lax.dynamic_index_in_dim(owners, me, 0, keepdims=False)
    same = own_owner[:, None] == own_owner[None, :]
    earlier = jnp.arange(windows)[None, :] < jnp.arange(windows)[:, None]
    own_rank = jnp.sum((same & earlier).astype(jnp.int32), axis=1)
    return got.at[own_owner * capacity + own_rank].get(mode="promise_in_bounds")


def local(
    projected,
    cache_history,
    cache_inputs,
    feature_taps,
    filters,
    skip_weight,
    base_inputs,
    window_owner,
    window_slot,
    variant_position,
    allele,
):
    var_count, tp_count = lax.axis_size("var"), lax.axis_size("tp")
    me, part = lax.axis_index("var"), lax.axis_index("tp")
    windows, own = variant_position.shape[0], projected.shape[0]
    width = cache_history.shape[2]
    slots = cache_history.shape[0]
    group_size = width // filters.shape[1]
    lead, carried, params = owner_of(
        cache_history,
        cache_inputs,
        filters.T,
        feature_taps.transpose(1, 0, 2),
        base_inputs.transpose(1, 0, 2),
        skip_weight[None],
        group_size,
    )
    packed = jnp.concatenate([lead, carried], axis=1)
    received = exchange(packed, window_owner, window_slot, me, windows)
    received = received.reshape(tp_count, own * received.shape[1], LANES)
    swapped = lax.all_to_all(received, "tp", split_axis=0, concat_axis=0, tiled=True)
    swapped = swapped.reshape(tp_count, own, -1, LANES)
    params = lax.all_gather(params, "tp", axis=0)
    cut = lead.shape[1]
    position = lax.dynamic_slice(variant_position, (part * own,), (own,))
    letter = lax.dynamic_slice(allele, (part * own,), (own,))
    taps, streams = feature_taps.shape[:2]
    return mixer_of(
        (taps, base_inputs.shape[0], streams, cache_inputs.shape[1]),
        position,
        letter,
        projected.transpose(0, 2, 1, 3),
        swapped[:, :, :cut],
        swapped[:, :, cut:],
        params,
    )


def solution(mesh):
    return jax.shard_map(
        local,
        mesh=mesh,
        in_specs=(
            P(("var", "tp"), None, None, None),
            P("var", None, "tp"),
            P("var", None, None, "tp"),
            P(None, None, "tp"),
            P(None, "tp"),
            P("tp"),
            P(None, None, "tp"),
            P(),
            P(),
            P("var"),
            P("var"),
        ),
        out_specs=P(("var", "tp"), None, None),
        check_vma=False,
    )
```

```python
import functools
import math
import jax
import jax.numpy as jnp
from jax import lax
from jax.experimental import pallas as pl
from jax.experimental.pallas import tpu as pltpu
from jax.sharding import PartitionSpec as P

LANES = 128
TAP_ROWS = 24
BASE_ROWS = 16
CAPACITY = 2
TIME = 32


def lead_kernel(pick_ref, inputs_ref, send_ref, rows_scr, lead_scr):
    loci, lead_len, streams, width = inputs_ref.shape
    blocks = width // LANES
    for n in range(loci):
        for r in range(lead_len):
            for b in range(blocks):
                at = ((n * blocks + b) * lead_len + r) * streams
                piece = inputs_ref[n, r, :, b * LANES : (b + 1) * LANES]
                rows_scr[at : at + streams, :] = piece.astype(jnp.float32)
    span = blocks * lead_len * streams
    for n in range(loci):
        lead_scr[n] = rows_scr[n * span : (n + 1) * span, :].astype(jnp.bfloat16)

    def copy(i, carry):
        send_ref[i] = lead_scr[pick_ref[i]]
        return carry

    lax.fori_loop(0, send_ref.shape[0], copy, 0, unroll=8)


def lead_of(pick, inputs):
    loci, lead_len, streams, width = inputs.shape
    rows = width // LANES * lead_len * streams
    return pl.pallas_call(
        lead_kernel,
        out_shape=jax.ShapeDtypeStruct((pick.shape[0], rows, LANES), jnp.bfloat16),
        in_specs=[pl.BlockSpec(memory_space=pltpu.SMEM), pl.BlockSpec(memory_space=pltpu.VMEM)],
        out_specs=pl.BlockSpec(memory_space=pltpu.VMEM),
        scratch_shapes=[
            pltpu.VMEM((loci * rows, LANES), jnp.float32),
            pltpu.VMEM((loci, rows, LANES), jnp.bfloat16),
        ],
        name="lead",
    )(pick, inputs)


def owner_kernel(group_size, history_ref, filters_ref, carried_ref, line_scr):
    loci, history_len, width = history_ref.shape
    tap_count = filters_ref.shape[1]
    blocks = width // LANES
    per_block = LANES // group_size
    f32 = jnp.float32
    row = lax.broadcasted_iota(jnp.int32, (tap_count, tap_count), 0)
    col = lax.broadcasted_iota(jnp.int32, (tap_count, tap_count), 1)
    flip = (row + col == tap_count - 1).astype(jnp.bfloat16)
    line_scr[...] = jnp.dot(filters_ref[...], flip, preferred_element_type=f32)
    t_row = lax.broadcasted_iota(jnp.int32, (TIME, tap_count), 0)
    s_col = lax.broadcasted_iota(jnp.int32, (TIME, tap_count), 1)
    valid = (s_col >= t_row) & (s_col < history_len)
    lane = lax.broadcasted_iota(jnp.int32, (TIME, LANES), 1) // group_size
    for b in range(blocks):
        tables = []
        for g in range(per_block):
            index = b * per_block + g
            line = jnp.broadcast_to(line_scr[index : index + 1, :], (TIME, tap_count))
            turned = pltpu.roll(line, 0, 1, stride=1, stride_axis=0)
            tables.append(jnp.where(valid, turned, 0.0))
        table = jnp.concatenate(tables, axis=0).astype(jnp.bfloat16)[:, :history_len]
        for n in range(loci):
            past = history_ref[n, :, b * LANES : (b + 1) * LANES]
            full = jnp.dot(table, past, preferred_element_type=f32)
            total = jnp.zeros((TIME, LANES), f32)
            for g in range(per_block):
                total = jnp.where(lane == g, full[g * TIME : (g + 1) * TIME], total)
            carried_ref[n, b * TIME : (b + 1) * TIME, :] = total.astype(jnp.bfloat16)


def owner_of(history, filters_t, group_size):
    loci, _, width = history.shape
    return pl.pallas_call(
        functools.partial(owner_kernel, group_size),
        out_shape=jax.ShapeDtypeStruct((loci, width // LANES * TIME, LANES), jnp.bfloat16),
        in_specs=[pl.BlockSpec(memory_space=pltpu.VMEM)] * 2,
        out_specs=pl.BlockSpec(memory_space=pltpu.VMEM),
        scratch_shapes=[pltpu.VMEM(filters_t.shape, jnp.float32)],
        name="owner",
    )(history, filters_t)


def pack_kernel(own, row_ref, allele_ref, got_ref, taps_ref, base_ref, skip_ref, filters_ref,
                out_ref, par_scr, base_scr):
    parts = out_ref.shape[0]
    lead_rows = got_ref.shape[1]
    streams, taps, width = taps_ref.shape
    bases = base_ref.shape[1]
    blocks = width // LANES
    groups = filters_ref.shape[0]
    f32 = jnp.float32
    par_scr[...] = jnp.zeros_like(par_scr)
    base_scr[...] = jnp.zeros_like(base_scr)
    for b in range(blocks):
        lanes = slice(b * LANES, (b + 1) * LANES)
        for s in range(streams):
            at = b * TAP_ROWS + s * taps
            par_scr[at : at + taps, :] = taps_ref[s, :, lanes].astype(f32)
            for letter in range(bases):
                at = letter * BASE_ROWS + b * streams + s
                base_scr[at : at + 1, :] = base_ref[s, letter : letter + 1, lanes].astype(f32)
        at = b * TAP_ROWS + streams * taps
        par_scr[at : at + 1, :] = skip_ref[:, lanes].astype(f32)
    par_rows = blocks * TAP_ROWS
    first = own * lead_rows

    def fill(k, carry):
        for w in range(own):
            out_ref[k, w * lead_rows : (w + 1) * lead_rows, :] = got_ref[row_ref[k * own + w]]
        out_ref[k, first : first + par_rows, :] = par_scr[...].astype(jnp.bfloat16)
        out_ref[k, first + par_rows : first + par_rows + groups, :] = filters_ref[...]
        for w in range(own):
            at = first + par_rows + groups + w * BASE_ROWS
            source = pl.multiple_of(allele_ref[k * own + w] * BASE_ROWS, BASE_ROWS)
            piece = base_scr[pl.ds(source, BASE_ROWS), :]
            out_ref[k, at : at + BASE_ROWS, :] = piece.astype(jnp.bfloat16)
        return carry

    lax.fori_loop(0, parts, fill, 0)


def pack_of(own, row, allele, got, taps, base, skip, filters_t):
    parts = row.shape[0] // own
    blocks = taps.shape[2] // LANES
    rows = own * (got.shape[1] + BASE_ROWS) + blocks * TAP_ROWS + filters_t.shape[0]
    return pl.pallas_call(
        functools.partial(pack_kernel, own),
        out_shape=jax.ShapeDtypeStruct((parts, rows, LANES), jnp.bfloat16),
        in_specs=[pl.BlockSpec(memory_space=pltpu.SMEM)] * 2 + [pl.BlockSpec(memory_space=pltpu.VMEM)] * 5,
        out_specs=pl.BlockSpec(memory_space=pltpu.VMEM),
        scratch_shapes=[
            pltpu.VMEM((blocks * TAP_ROWS, LANES), jnp.float32),
            pltpu.VMEM((base.shape[1] * BASE_ROWS, LANES), jnp.float32),
        ],
        name="pack",
    )(row, allele, got, taps, base, skip, filters_t)


def mixer_kernel(dims, pos_ref, proj_ref, pack_ref, gate_ref, part_ref,
                 x_scr, l_scr, p_scr, f_scr, b_scr, m_scr):
    taps, lead_len, groups = dims
    wins, streams, _, width = proj_ref.shape
    blocks = width // LANES
    rows = wins * blocks
    lead_rows = lead_len * streams
    f32 = jnp.float32
    span = blocks * lead_rows
    first = wins * span
    par_rows = blocks * TAP_ROWS
    spread_row = lax.broadcasted_iota(jnp.int32, (groups, width), 0)
    spread_col = lax.broadcasted_iota(jnp.int32, (groups, width), 1) // (width // groups)
    spread = (spread_row == spread_col).astype(jnp.bfloat16)
    filt = pack_ref[0, first + par_rows : first + par_rows + groups, :]
    wide = lax.dot_general(filt, spread, (((0,), (0,)), ((), ())), preferred_element_type=f32)
    for w in range(wins):
        l_scr[w * span : (w + 1) * span, :] = pack_ref[0, w * span : (w + 1) * span, :].astype(f32)
        p_scr[w * par_rows : (w + 1) * par_rows, :] = pack_ref[0, first : first + par_rows, :].astype(f32)
        at = first + par_rows + groups + w * BASE_ROWS
        b_scr[w * BASE_ROWS : (w + 1) * BASE_ROWS, :] = pack_ref[0, at : at + BASE_ROWS, :].astype(f32)
        for b in range(blocks):
            q = w * blocks + b
            lanes = slice(b * LANES, (b + 1) * LANES)
            f_scr[q * TIME : (q + 1) * TIME, :] = wide[:TIME, lanes]
            for s in range(streams):
                x_scr[s, q * TIME : (q + 1) * TIME, :] = proj_ref[w, s, :, lanes].astype(f32)
    for w in range(wins):
        for s in range(streams):
            for b in range(blocks):
                q = w * blocks + b
                source = w * BASE_ROWS + b * streams + s
                x_scr[s, pl.ds(q * TIME + pos_ref[w], 1), :] = b_scr[source : source + 1, :]

    def param(r):
        return p_scr[pl.ds(r, rows, stride=TAP_ROWS), :]

    def entry(s, r):
        if r < lead_len:
            return l_scr[pl.ds(r * streams + s, rows, stride=lead_rows), :]
        return x_scr[s, pl.ds(r - lead_len, rows, stride=TIME), :]

    def featured(s):
        weight = [param(s * taps + j) for j in range(taps)]
        window = [entry(s, r) for r in range(taps - 1)]
        for t in range(TIME):
            window.append(entry(s, t + taps - 1))
            total = weight[0] * window[taps - 1]
            for j in range(1, taps):
                total = total + weight[j] * window[taps - 1 - j]
            window.pop(0)
            yield total

    for t, (one, two) in enumerate(zip(featured(1), featured(2))):
        m_scr[t] = (one * two).astype(jnp.bfloat16).astype(f32)
    skip = param(streams * taps)
    for t, gate in enumerate(featured(0)):
        gate_ref[0, pl.ds(t, rows, stride=TIME), :] = gate
    step = 8
    for start in range(0, TIME, step):
        total = [None] * step
        for j in range(start + step):
            tap = f_scr[pl.ds(j, rows, stride=TIME), :]
            for i in range(step):
                at = start + i - j
                if at >= 0:
                    term = tap * m_scr[at]
                    total[i] = term if total[i] is None else total[i] + term
        for i in range(step):
            t = start + i
            part_ref[0, pl.ds(t, rows, stride=TIME), :] = total[i] + skip * m_scr[t]


def mixer_of(dims, position, proj, packed):
    wins, streams, _, total = proj.shape
    parts = packed.shape[0]
    width = total // parts
    blocks = width // LANES
    rows = wins * blocks
    lead_rows = dims[1] * streams
    shape = jax.ShapeDtypeStruct((parts, rows * TIME, LANES), jnp.float32)
    out_spec = pl.BlockSpec((1, rows * TIME, LANES), lambda k, *_: (k, 0, 0))
    return pl.pallas_call(
        functools.partial(mixer_kernel, dims),
        out_shape=(shape, shape),
        grid_spec=pltpu.PrefetchScalarGridSpec(
            num_scalar_prefetch=1,
            grid=(parts,),
            in_specs=[
                pl.BlockSpec((wins, streams, TIME, width), lambda k, *_: (0, 0, 0, k)),
                pl.BlockSpec((1,) + packed.shape[1:], lambda k, *_: (k, 0, 0)),
            ],
            out_specs=[out_spec, out_spec],
            scratch_shapes=[
                pltpu.VMEM((streams, rows * TIME, LANES), jnp.float32),
                pltpu.VMEM((rows * lead_rows, LANES), jnp.float32),
                pltpu.VMEM((rows * TAP_ROWS, LANES), jnp.float32),
                pltpu.VMEM((rows * TIME, LANES), jnp.float32),
                pltpu.VMEM((wins * BASE_ROWS, LANES), jnp.float32),
                pltpu.VMEM((TIME, rows, LANES), jnp.float32),
            ],
        ),
        cost_estimate=pl.CostEstimate(flops=2 * 10**9, bytes_accessed=10 * 2**20, transcendentals=0),
        name="mixer",
    )(position, proj, packed)


def combine_kernel(gate_ref, part_ref, carried_ref, out_ref):
    parts, rows, _ = gate_ref.shape
    wins, _, total = out_ref.shape
    blocks = rows // TIME // wins
    width = total // parts

    def body(k, carry):
        for w in range(wins):
            for b in range(blocks):
                at = slice((w * blocks + b) * TIME, (w * blocks + b + 1) * TIME)
                lanes = pl.ds(pl.multiple_of(k * width + b * LANES, LANES), LANES)
                filtered = part_ref[k, at, :] + carried_ref[k, at, :].astype(jnp.float32)
                out_ref[w, :, lanes] = (gate_ref[k, at, :] * filtered).astype(jnp.bfloat16)
        return carry

    lax.fori_loop(0, parts, body, 0)


def combine_of(gate, part, carried, wins):
    parts, rows, _ = gate.shape
    width = rows // TIME // wins * LANES
    return pl.pallas_call(
        combine_kernel,
        out_shape=jax.ShapeDtypeStruct((wins, TIME, parts * width), jnp.bfloat16),
        in_specs=[pl.BlockSpec(memory_space=pltpu.VMEM)] * 3,
        out_specs=pl.BlockSpec(memory_space=pltpu.VMEM),
        name="combine",
    )(gate, part, carried)


def rank_of(keys):
    count = keys.shape[-1]
    same = keys[..., :, None] == keys[..., None, :]
    earlier = jnp.arange(count)[None, :] < jnp.arange(count)[:, None]
    return jnp.sum((same & earlier).astype(jnp.int32), axis=-1)


def slots_of(mask, values, capacity):
    rank = jnp.cumsum(mask.astype(jnp.int32), axis=-1) - 1
    hit = mask[..., None, :] & (rank[..., None, :] == jnp.arange(capacity)[:, None])
    return jnp.sum(jnp.where(hit, values[..., None, :], 0), axis=-1)


def take_rows(array, index):
    return array.at[index].get(mode="promise_in_bounds")


def local(
    grid_y,
    projected,
    cache_history,
    cache_inputs,
    feature_taps,
    filters,
    skip_weight,
    base_inputs,
    window_owner,
    window_slot,
    variant_position,
    allele,
):
    var_count, tp_count = lax.axis_size("var"), lax.axis_size("tp")
    me, part = lax.axis_index("var"), lax.axis_index("tp")
    grid_x = var_count // grid_y
    my_x, my_y = me // grid_y, me % grid_y
    windows, own = variant_position.shape[0], projected.shape[0]
    loci, _, width = cache_history.shape
    group_size = width // filters.shape[1]
    taps, streams = feature_taps.shape[:2]
    lead_len = cache_inputs.shape[1]
    filters_t = filters.T

    owners = window_owner[:, 0].reshape(var_count, windows)
    slots = window_slot.reshape(var_count, windows)
    pick = slots_of(owners == me, slots, CAPACITY).reshape(-1)
    lead_send = lead_of(pick, cache_inputs)
    lead_send = lead_send.reshape(var_count, -1, LANES)
    lead_got = lax.all_to_all(lead_send, "var", split_axis=0, concat_axis=0, tiled=True)
    lead_got = lead_got.reshape(var_count * CAPACITY, -1, LANES)

    carried = owner_of(cache_history, filters_t, group_size)

    def ring(shift):
        return [(x * grid_y + y, x * grid_y + (y + shift) % grid_y) for x in range(grid_x) for y in range(grid_y)]

    ahead, back = [carried], [carried]
    for hop in range(grid_y // 2):
        ahead.append(lax.ppermute(ahead[-1], "var", ring(1)))
        if hop < (grid_y - 1) // 2:
            back.append(lax.ppermute(back[-1], "var", ring(-1)))
    lead_got, _, _ = lax.optimization_barrier((lead_got, ahead[-1], back[-1]))
    column = jnp.concatenate(ahead + back[:0:-1], axis=0)

    reach = min(windows, CAPACITY * grid_y)
    targets = (my_x + jnp.arange(grid_x)) % grid_x * grid_y + my_y
    their_owners, their_slots = owners[targets], slots[targets]
    spot = (my_y - their_owners % grid_y) % grid_y * loci + their_slots
    wanted = slots_of(their_owners // grid_y == my_x, spot, reach)

    own_owner = lax.dynamic_index_in_dim(owners, me, 0, keepdims=False)
    own_x = own_owner // grid_y
    own_row = (my_x - own_x) % grid_x * reach + rank_of(own_x)
    lead_row = own_owner * CAPACITY + rank_of(own_owner)

    def across(shift):
        return [(x * grid_y + y, (x + shift) % grid_x * grid_y + y) for x in range(grid_x) for y in range(grid_y)]

    packed = pack_of(
        own,
        lead_row,
        allele,
        lead_got,
        feature_taps.transpose(1, 0, 2),
        base_inputs.transpose(1, 0, 2),
        skip_weight[None],
        filters_t,
    )
    packed = lax.all_to_all(packed, "tp", split_axis=0, concat_axis=0, tiled=True)

    arrived = [take_rows(column, wanted[0])]
    for shift in range(1, grid_x):
        arrived.append(lax.ppermute(take_rows(column, wanted[shift]), "var", across(shift)))
    mine = take_rows(jnp.concatenate(arrived, axis=0), own_row)
    mine = mine.reshape(tp_count, -1, LANES)
    mine = lax.all_to_all(mine, "tp", split_axis=0, concat_axis=0, tiled=True)

    position = lax.dynamic_slice(variant_position, (part * own,), (own,))
    gate, partial = mixer_of(
        (taps, lead_len, filters_t.shape[0]), position, projected.transpose(0, 2, 1, 3), packed
    )
    return combine_of(gate, partial, mine, own)


def solution(mesh):
    grid_y = math.gcd(mesh.shape["var"], 8)
    return jax.shard_map(
        functools.partial(local, grid_y),
        mesh=mesh,
        in_specs=(
            P(("var", "tp"), None, None, None),
            P("var", None, "tp"),
            P("var", None, None, "tp"),
            P(None, None, "tp"),
            P(None, "tp"),
            P("tp"),
            P(None, None, "tp"),
            P(),
            P(),
            P("var"),
            P("var"),
        ),
        out_specs=P(("var", "tp"), None, None),
        check_vma=False,
    )
```

```python
import functools
import jax
import jax.numpy as jnp
from jax import lax
from jax.experimental import pallas as pl
from jax.experimental.pallas import tpu as pltpu
from jax.sharding import PartitionSpec as P

LANES = 128
TAP_ROWS = 24
BASE_ROWS = 16
CAPACITY = 2
TIME = 32


def lead_kernel(pick_ref, inputs_ref, send_ref, rows_scr, lead_scr):
    loci, lead_len, streams, width = inputs_ref.shape
    blocks = width // LANES
    for n in range(loci):
        for r in range(lead_len):
            for b in range(blocks):
                at = ((n * blocks + b) * lead_len + r) * streams
                piece = inputs_ref[n, r, :, b * LANES : (b + 1) * LANES]
                rows_scr[at : at + streams, :] = piece.astype(jnp.float32)
    span = blocks * lead_len * streams
    for n in range(loci):
        lead_scr[n] = rows_scr[n * span : (n + 1) * span, :].astype(jnp.bfloat16)

    def copy(i, carry):
        send_ref[i] = lead_scr[pick_ref[i]]
        return carry

    lax.fori_loop(0, send_ref.shape[0], copy, 0, unroll=8)


def lead_of(pick, inputs):
    loci, lead_len, streams, width = inputs.shape
    rows = width // LANES * lead_len * streams
    return pl.pallas_call(
        lead_kernel,
        out_shape=jax.ShapeDtypeStruct((pick.shape[0], rows, LANES), jnp.bfloat16),
        in_specs=[pl.BlockSpec(memory_space=pltpu.SMEM), pl.BlockSpec(memory_space=pltpu.VMEM)],
        out_specs=pl.BlockSpec(memory_space=pltpu.VMEM),
        scratch_shapes=[
            pltpu.VMEM((loci * rows, LANES), jnp.float32),
            pltpu.VMEM((loci, rows, LANES), jnp.bfloat16),
        ],
        name="lead",
    )(pick, inputs)


def owner_kernel(group_size, history_ref, filters_ref, carried_ref, line_scr):
    loci, history_len, width = history_ref.shape
    tap_count = filters_ref.shape[1]
    blocks = width // LANES
    per_block = LANES // group_size
    f32 = jnp.float32
    row = lax.broadcasted_iota(jnp.int32, (tap_count, tap_count), 0)
    col = lax.broadcasted_iota(jnp.int32, (tap_count, tap_count), 1)
    flip = (row + col == tap_count - 1).astype(jnp.bfloat16)
    line_scr[...] = jnp.dot(filters_ref[...], flip, preferred_element_type=f32)
    t_row = lax.broadcasted_iota(jnp.int32, (TIME, tap_count), 0)
    s_col = lax.broadcasted_iota(jnp.int32, (TIME, tap_count), 1)
    valid = (s_col >= t_row) & (s_col < history_len)
    lane = lax.broadcasted_iota(jnp.int32, (TIME, LANES), 1) // group_size
    for b in range(blocks):
        tables = []
        for g in range(per_block):
            index = b * per_block + g
            line = jnp.broadcast_to(line_scr[index : index + 1, :], (TIME, tap_count))
            turned = pltpu.roll(line, 0, 1, stride=1, stride_axis=0)
            tables.append(jnp.where(valid, turned, 0.0))
        table = jnp.concatenate(tables, axis=0).astype(jnp.bfloat16)[:, :history_len]
        for n in range(loci):
            past = history_ref[n, :, b * LANES : (b + 1) * LANES]
            full = jnp.dot(table, past, preferred_element_type=f32)
            total = jnp.zeros((TIME, LANES), f32)
            for g in range(per_block):
                total = jnp.where(lane == g, full[g * TIME : (g + 1) * TIME], total)
            carried_ref[n, b * TIME : (b + 1) * TIME, :] = total.astype(jnp.bfloat16)


def owner_of(history, filters_t, group_size):
    loci, _, width = history.shape
    return pl.pallas_call(
        functools.partial(owner_kernel, group_size),
        out_shape=jax.ShapeDtypeStruct((loci, width // LANES * TIME, LANES), jnp.bfloat16),
        in_specs=[pl.BlockSpec(memory_space=pltpu.VMEM)] * 2,
        out_specs=pl.BlockSpec(memory_space=pltpu.VMEM),
        scratch_shapes=[pltpu.VMEM(filters_t.shape, jnp.float32)],
        name="owner",
    )(history, filters_t)


def params_kernel(taps_ref, skip_ref, filters_ref, out_ref, par_scr):
    streams, taps, width = taps_ref.shape
    f32 = jnp.float32
    par_scr[...] = jnp.zeros_like(par_scr)
    for b in range(width // LANES):
        lanes = slice(b * LANES, (b + 1) * LANES)
        for s in range(streams):
            at = b * TAP_ROWS + s * taps
            par_scr[at : at + taps, :] = taps_ref[s, :, lanes].astype(f32)
        at = b * TAP_ROWS + streams * taps
        par_scr[at : at + 1, :] = skip_ref[:, lanes].astype(f32)
    rows = par_scr.shape[0]
    out_ref[:rows, :] = par_scr[...].astype(jnp.bfloat16)
    out_ref[rows:, :] = filters_ref[...]


def params_of(taps, skip, filters_t):
    rows = taps.shape[2] // LANES * TAP_ROWS
    return pl.pallas_call(
        params_kernel,
        out_shape=jax.ShapeDtypeStruct((rows + filters_t.shape[0], LANES), jnp.bfloat16),
        in_specs=[pl.BlockSpec(memory_space=pltpu.VMEM)] * 3,
        out_specs=pl.BlockSpec(memory_space=pltpu.VMEM),
        scratch_shapes=[pltpu.VMEM((rows, LANES), jnp.float32)],
        name="params",
    )(taps, skip, filters_t)


def pack_kernel(own, row_ref, allele_ref, order_ref, got_ref, base_ref, near_ref, far_ref, base_scr):
    half = near_ref.shape[0]
    lead_rows = got_ref.shape[1]
    streams, bases, width = base_ref.shape
    base_scr[...] = jnp.zeros_like(base_scr)
    for b in range(width // LANES):
        for s in range(streams):
            for letter in range(bases):
                at = letter * BASE_ROWS + b * streams + s
                piece = base_ref[s, letter : letter + 1, b * LANES : (b + 1) * LANES]
                base_scr[at : at + 1, :] = piece.astype(jnp.float32)
    first = own * lead_rows
    for half_index, out_ref in enumerate((near_ref, far_ref)):

        def fill(i, carry):
            k = order_ref[half_index * half + i]
            for w in range(own):
                out_ref[i, w * lead_rows : (w + 1) * lead_rows, :] = got_ref[row_ref[k * own + w]]
                at = first + w * BASE_ROWS
                source = pl.multiple_of(allele_ref[k * own + w] * BASE_ROWS, BASE_ROWS)
                piece = base_scr[pl.ds(source, BASE_ROWS), :]
                out_ref[i, at : at + BASE_ROWS, :] = piece.astype(jnp.bfloat16)
            return carry

        lax.fori_loop(0, half, fill, 0)


def pack_of(own, row, allele, order, got, base):
    rows = own * (got.shape[1] + BASE_ROWS)
    half = jax.ShapeDtypeStruct((order.shape[0] // 2, rows, LANES), jnp.bfloat16)
    return pl.pallas_call(
        functools.partial(pack_kernel, own),
        out_shape=(half, half),
        in_specs=[pl.BlockSpec(memory_space=pltpu.SMEM)] * 3 + [pl.BlockSpec(memory_space=pltpu.VMEM)] * 2,
        out_specs=[pl.BlockSpec(memory_space=pltpu.VMEM)] * 2,
        scratch_shapes=[pltpu.VMEM((base.shape[1] * BASE_ROWS, LANES), jnp.float32)],
        name="pack",
    )(row, allele, order, got, base)


def mixer_kernel(dims, pos_ref, order_ref, proj_ref, pack_ref, par_ref, gate_ref, part_ref,
                 x_scr, l_scr, p_scr, f_scr, b_scr, m_scr):
    taps, lead_len, groups = dims
    place = order_ref[pl.program_id(0)]
    wins, streams, _, width = proj_ref.shape
    blocks = width // LANES
    rows = wins * blocks
    lead_rows = lead_len * streams
    f32 = jnp.float32
    span = blocks * lead_rows
    first = wins * span
    par_rows = blocks * TAP_ROWS
    spread_row = lax.broadcasted_iota(jnp.int32, (groups, width), 0)
    spread_col = lax.broadcasted_iota(jnp.int32, (groups, width), 1) // (width // groups)
    spread = (spread_row == spread_col).astype(jnp.bfloat16)
    filt = par_ref[0, par_rows : par_rows + groups, :]
    wide = lax.dot_general(filt, spread, (((0,), (0,)), ((), ())), preferred_element_type=f32)
    for w in range(wins):
        l_scr[w * span : (w + 1) * span, :] = pack_ref[0, w * span : (w + 1) * span, :].astype(f32)
        p_scr[w * par_rows : (w + 1) * par_rows, :] = par_ref[0, :par_rows, :].astype(f32)
        at = first + w * BASE_ROWS
        b_scr[w * BASE_ROWS : (w + 1) * BASE_ROWS, :] = pack_ref[0, at : at + BASE_ROWS, :].astype(f32)
        for b in range(blocks):
            q = w * blocks + b
            lanes = slice(b * LANES, (b + 1) * LANES)
            f_scr[q * TIME : (q + 1) * TIME, :] = wide[:TIME, lanes]
            for s in range(streams):
                x_scr[s, q * TIME : (q + 1) * TIME, :] = proj_ref[w, s, :, lanes].astype(f32)
    for w in range(wins):
        for s in range(streams):
            for b in range(blocks):
                q = w * blocks + b
                source = w * BASE_ROWS + b * streams + s
                x_scr[s, pl.ds(q * TIME + pos_ref[w], 1), :] = b_scr[source : source + 1, :]

    def param(r):
        return p_scr[pl.ds(r, rows, stride=TAP_ROWS), :]

    def entry(s, r):
        if r < lead_len:
            return l_scr[pl.ds(r * streams + s, rows, stride=lead_rows), :]
        return x_scr[s, pl.ds(r - lead_len, rows, stride=TIME), :]

    def featured(s):
        weight = [param(s * taps + j) for j in range(taps)]
        window = [entry(s, r) for r in range(taps - 1)]
        for t in range(TIME):
            window.append(entry(s, t + taps - 1))
            total = weight[0] * window[taps - 1]
            for j in range(1, taps):
                total = total + weight[j] * window[taps - 1 - j]
            window.pop(0)
            yield total

    for t, (one, two) in enumerate(zip(featured(1), featured(2))):
        m_scr[t] = (one * two).astype(jnp.bfloat16).astype(f32)
    skip = param(streams * taps)
    for t, gate in enumerate(featured(0)):
        gate_ref[place, pl.ds(t, rows, stride=TIME), :] = gate
    step = 8
    for start in range(0, TIME, step):
        total = [None] * step
        for j in range(start + step):
            tap = f_scr[pl.ds(j, rows, stride=TIME), :]
            for i in range(step):
                at = start + i - j
                if at >= 0:
                    term = tap * m_scr[at]
                    total[i] = term if total[i] is None else total[i] + term
        for i in range(step):
            t = start + i
            part_ref[place, pl.ds(t, rows, stride=TIME), :] = total[i] + skip * m_scr[t]


def mixer_of(dims, position, order, proj, packed, params):
    wins, streams, _, total = proj.shape
    parts = packed.shape[0]
    width = total // parts
    blocks = width // LANES
    rows = wins * blocks
    lead_rows = dims[1] * streams
    shape = pltpu.VMEM((parts, rows * TIME, LANES), jnp.float32)
    out_spec = pl.BlockSpec(memory_space=pltpu.VMEM)
    return pl.pallas_call(
        functools.partial(mixer_kernel, dims),
        out_shape=(shape, shape),
        grid_spec=pltpu.PrefetchScalarGridSpec(
            num_scalar_prefetch=2,
            grid=(parts,),
            in_specs=[
                pl.BlockSpec((wins, streams, TIME, width), lambda k, pos, order: (0, 0, 0, order[k])),
                pl.BlockSpec((1,) + packed.shape[1:], lambda k, *_: (k, 0, 0)),
                pl.BlockSpec((1,) + params.shape[1:], lambda k, pos, order: (order[k], 0, 0)),
            ],
            out_specs=[out_spec, out_spec],
            scratch_shapes=[
                pltpu.VMEM((streams, rows * TIME, LANES), jnp.float32),
                pltpu.VMEM((rows * lead_rows, LANES), jnp.float32),
                pltpu.VMEM((rows * TAP_ROWS, LANES), jnp.float32),
                pltpu.VMEM((rows * TIME, LANES), jnp.float32),
                pltpu.VMEM((wins * BASE_ROWS, LANES), jnp.float32),
                pltpu.VMEM((TIME, rows, LANES), jnp.float32),
            ],
        ),
        compiler_params=pltpu.CompilerParams(vmem_limit_bytes=24 * 2**20),
        cost_estimate=pl.CostEstimate(flops=2 * 10**9, bytes_accessed=10 * 2**20, transcendentals=0),
        name="mixer",
    )(position, order, proj, packed, params)


def combine_kernel(gate_ref, part_ref, carried_ref, out_ref):
    parts, rows, _ = gate_ref.shape
    wins, _, total = out_ref.shape
    blocks = rows // TIME // wins
    width = total // parts

    def body(k, carry):
        for w in range(wins):
            for b in range(blocks):
                at = slice((w * blocks + b) * TIME, (w * blocks + b + 1) * TIME)
                lanes = pl.ds(pl.multiple_of(k * width + b * LANES, LANES), LANES)
                filtered = part_ref[k, at, :] + carried_ref[k, at, :].astype(jnp.float32)
                out_ref[w, :, lanes] = (gate_ref[k, at, :] * filtered).astype(jnp.bfloat16)
        return carry

    lax.fori_loop(0, parts, body, 0)


def combine_of(gate, part, carried, wins):
    parts, rows, _ = gate.shape
    width = rows // TIME // wins * LANES
    return pl.pallas_call(
        combine_kernel,
        out_shape=jax.ShapeDtypeStruct((wins, TIME, parts * width), jnp.bfloat16),
        in_specs=[pl.BlockSpec(memory_space=pltpu.VMEM)] * 3,
        out_specs=pl.BlockSpec(memory_space=pltpu.VMEM),
        compiler_params=pltpu.CompilerParams(vmem_limit_bytes=24 * 2**20),
        name="combine",
    )(gate, part, pltpu.with_memory_space_constraint(carried, pltpu.VMEM))


def rank_of(keys):
    count = keys.shape[-1]
    same = keys[..., :, None] == keys[..., None, :]
    earlier = jnp.arange(count)[None, :] < jnp.arange(count)[:, None]
    return jnp.sum((same & earlier).astype(jnp.int32), axis=-1)


def slots_of(mask, values, capacity):
    rank = jnp.cumsum(mask.astype(jnp.int32), axis=-1) - 1
    hit = mask[..., None, :] & (rank[..., None, :] == jnp.arange(capacity)[:, None])
    return jnp.sum(jnp.where(hit, values[..., None, :], 0), axis=-1)


def take_rows(array, index):
    return array.at[index].get(mode="promise_in_bounds")


def local(
    projected,
    cache_history,
    cache_inputs,
    feature_taps,
    filters,
    skip_weight,
    base_inputs,
    window_owner,
    window_slot,
    variant_position,
    allele,
):
    var_count, tp_count = lax.axis_size("var"), lax.axis_size("tp")
    me, part = lax.axis_index("var"), lax.axis_index("tp")
    windows, own = variant_position.shape[0], projected.shape[0]
    loci, _, width = cache_history.shape
    group_size = width // filters.shape[1]
    taps, streams = feature_taps.shape[:2]
    lead_len = cache_inputs.shape[1]
    filters_t = filters.T

    owners = window_owner.reshape(var_count, windows)
    slots = window_slot.reshape(var_count, windows)
    pick = slots_of(owners == me, slots, CAPACITY).reshape(-1)
    own_owner = lax.dynamic_index_in_dim(owners, me, 0, keepdims=False)
    own_row = own_owner * CAPACITY + rank_of(own_owner)

    def exchange(rows):
        got = lax.all_to_all(rows.reshape(var_count, -1, LANES), "var", split_axis=0, concat_axis=0, tiled=True)
        return got.reshape(rows.shape)

    lead = exchange(lead_of(pick, cache_inputs))
    carried = take_rows(owner_of(cache_history, filters_t, group_size), pick)
    params = params_of(feature_taps.transpose(1, 0, 2), skip_weight[None], filters_t)
    params = lax.all_gather(params, "tp", axis=0)
    carried, lead, params = lax.optimization_barrier((carried, lead, params))
    carried = exchange(carried)

    half = tp_count // 2
    line, core = part // 2, part % 2
    steps = jnp.arange(half)
    targets = (line + steps) % half * 2
    near, far = pack_of(
        own,
        own_row,
        allele,
        jnp.concatenate([targets + core, targets + 1 - core]),
        lead,
        base_inputs.transpose(1, 0, 2),
    )
    other = lax.ppermute(far, "tp", [(k, k ^ 1) for k in range(tp_count)])
    both = [jnp.stack([near[step], other[step]]) for step in range(half)]
    for step in sorted(range(1, half), key=lambda step: -min(step, half - step)):
        both[step] = lax.ppermute(both[step], "tp", [(k, (k + 2 * step) % tp_count) for k in range(tp_count)])
    packed = jnp.concatenate(both, axis=0)
    sources = (line - steps) % half * 2
    order = jnp.stack([sources + core, sources + 1 - core], axis=1).reshape(-1)

    carried, _ = lax.optimization_barrier((carried, packed))
    carried = take_rows(carried, own_row).reshape(tp_count, -1, LANES)
    carried = lax.all_to_all(carried, "tp", split_axis=0, concat_axis=0, tiled=True)

    position = lax.dynamic_slice(variant_position, (part * own,), (own,))
    gate, partial = mixer_of(
        (taps, lead_len, filters_t.shape[0]), position, order, projected.transpose(0, 2, 1, 3), packed, params
    )
    return combine_of(gate, partial, carried, own)


def solution(mesh):
    return jax.shard_map(
        local,
        mesh=mesh,
        in_specs=(
            P(("var", "tp"), None, None, None),
            P("var", None, "tp"),
            P("var", None, None, "tp"),
            P(None, None, "tp"),
            P(None, "tp"),
            P("tp"),
            P(None, None, "tp"),
            P(),
            P(),
            P("var"),
            P("var"),
        ),
        out_specs=P(("var", "tp"), None, None),
        check_vma=False,
    )
```

```python
import functools
import jax
import jax.numpy as jnp
from jax import lax
from jax.experimental import pallas as pl
from jax.experimental.pallas import tpu as pltpu
from jax.sharding import PartitionSpec as P

LANES = 128
TAP_ROWS = 24
BASE_ROWS = 16
CAPACITY = 2
TIME = 32


def lead_kernel(windows, me_ref, owner_ref, slot_ref, inputs_ref, send_ref, rows_scr):
    loci, lead_len, streams, width = inputs_ref.shape
    blocks = width // LANES
    f32 = jnp.float32
    for n in range(loci):
        for r in range(lead_len):
            for b in range(blocks):
                at = ((n * blocks + b) * lead_len + r) * streams
                piece = inputs_ref[n, r, :, b * LANES : (b + 1) * LANES]
                rows_scr[at : at + streams, :] = piece.astype(f32)
    lanes = owner_ref.shape[1]
    row = lax.broadcasted_iota(jnp.int32, (lanes, lanes), 0)
    col = lax.broadcasted_iota(jnp.int32, (lanes, lanes), 1)
    before = ((row // windows == col // windows) & (row < col)).astype(jnp.bfloat16)
    gather = (row // windows == col).astype(jnp.bfloat16)
    mine = owner_ref[...] == me_ref[0]
    rank = jnp.dot(mine.astype(f32).astype(jnp.bfloat16), before, preferred_element_type=f32)
    slot = slot_ref[...].astype(f32)
    span = blocks * lead_len * streams
    segments = lanes // windows
    picks = []
    for r in range(CAPACITY):
        value = jnp.where(mine & (rank == r), slot, 0.0).astype(jnp.bfloat16)
        picks.append(jnp.dot(value, gather, preferred_element_type=f32))
    for i in range(send_ref.shape[0]):
        target, r = i // CAPACITY, i % CAPACITY
        pick = picks[r][target // segments : target // segments + 1, target % segments : target % segments + 1]
        pick = jnp.broadcast_to(pick, (span, LANES))
        found = rows_scr[:span, :]
        for n in range(1, loci):
            found = jnp.where(pick == n, rows_scr[n * span : (n + 1) * span, :], found)
        send_ref[i] = found.astype(jnp.bfloat16)


def lead_of(me, owners, slots, inputs, windows):
    loci, lead_len, streams, width = inputs.shape
    rows = width // LANES * lead_len * streams
    targets = slots.shape[0] // windows
    lanes = min(LANES, slots.shape[0])
    return pl.pallas_call(
        functools.partial(lead_kernel, windows),
        out_shape=jax.ShapeDtypeStruct((targets * CAPACITY, rows, LANES), jnp.bfloat16),
        in_specs=[pl.BlockSpec(memory_space=pltpu.SMEM)] + [pl.BlockSpec(memory_space=pltpu.VMEM)] * 3,
        out_specs=pl.BlockSpec(memory_space=pltpu.VMEM),
        scratch_shapes=[pltpu.VMEM((loci * rows, LANES), jnp.float32)],
        name="lead",
    )(me.reshape(1), owners.reshape(-1, lanes), slots.reshape(-1, lanes), inputs)


def owner_kernel(group_size, history_ref, filters_ref, carried_ref, line_scr):
    loci, history_len, width = history_ref.shape
    tap_count = filters_ref.shape[1]
    blocks = width // LANES
    per_block = LANES // group_size
    f32 = jnp.float32
    row = lax.broadcasted_iota(jnp.int32, (tap_count, tap_count), 0)
    col = lax.broadcasted_iota(jnp.int32, (tap_count, tap_count), 1)
    flip = (row + col == tap_count - 1).astype(jnp.bfloat16)
    line_scr[...] = jnp.dot(filters_ref[...], flip, preferred_element_type=f32)
    t_row = lax.broadcasted_iota(jnp.int32, (TIME, tap_count), 0)
    s_col = lax.broadcasted_iota(jnp.int32, (TIME, tap_count), 1)
    valid = (s_col >= t_row) & (s_col < history_len)
    lane = lax.broadcasted_iota(jnp.int32, (TIME, LANES), 1) // group_size
    for b in range(blocks):
        tables = []
        for g in range(per_block):
            index = b * per_block + g
            line = jnp.broadcast_to(line_scr[index : index + 1, :], (TIME, tap_count))
            turned = pltpu.roll(line, 0, 1, stride=1, stride_axis=0)
            tables.append(jnp.where(valid, turned, 0.0))
        table = jnp.concatenate(tables, axis=0).astype(jnp.bfloat16)[:, :history_len]
        for n in range(loci):
            past = history_ref[n, :, b * LANES : (b + 1) * LANES]
            full = jnp.dot(table, past, preferred_element_type=f32)
            total = jnp.zeros((TIME, LANES), f32)
            for g in range(per_block):
                total = jnp.where(lane == g, full[g * TIME : (g + 1) * TIME], total)
            carried_ref[n, b * TIME : (b + 1) * TIME, :] = total.astype(jnp.bfloat16)


def owner_of(history, filters_t, group_size):
    loci, _, width = history.shape
    return pl.pallas_call(
        functools.partial(owner_kernel, group_size),
        out_shape=jax.ShapeDtypeStruct((loci, width // LANES * TIME, LANES), jnp.bfloat16),
        in_specs=[pl.BlockSpec(memory_space=pltpu.VMEM)] * 2,
        out_specs=pl.BlockSpec(memory_space=pltpu.VMEM),
        scratch_shapes=[pltpu.VMEM(filters_t.shape, jnp.float32)],
        name="owner",
    )(history, filters_t)


def params_kernel(taps_ref, skip_ref, filters_ref, out_ref, par_scr):
    streams, taps, width = taps_ref.shape
    f32 = jnp.float32
    par_scr[...] = jnp.zeros_like(par_scr)
    for b in range(width // LANES):
        lanes = slice(b * LANES, (b + 1) * LANES)
        for s in range(streams):
            at = b * TAP_ROWS + s * taps
            par_scr[at : at + taps, :] = taps_ref[s, :, lanes].astype(f32)
        at = b * TAP_ROWS + streams * taps
        par_scr[at : at + 1, :] = skip_ref[:, lanes].astype(f32)
    rows = par_scr.shape[0]
    out_ref[:rows, :] = par_scr[...].astype(jnp.bfloat16)
    out_ref[rows:, :] = filters_ref[...]


def params_of(taps, skip, filters_t):
    rows = taps.shape[2] // LANES * TAP_ROWS
    return pl.pallas_call(
        params_kernel,
        out_shape=jax.ShapeDtypeStruct((rows + filters_t.shape[0], LANES), jnp.bfloat16),
        in_specs=[pl.BlockSpec(memory_space=pltpu.VMEM)] * 3,
        out_specs=pl.BlockSpec(memory_space=pltpu.VMEM),
        scratch_shapes=[pltpu.VMEM((rows, LANES), jnp.float32)],
        name="params",
    )(taps, skip, filters_t)


def pack_kernel(own, row_ref, allele_ref, order_ref, got_ref, base_ref, near_ref, far_ref, base_scr):
    half = near_ref.shape[0]
    lead_rows = got_ref.shape[1]
    streams, bases, width = base_ref.shape
    base_scr[...] = jnp.zeros_like(base_scr)
    for b in range(width // LANES):
        for s in range(streams):
            for letter in range(bases):
                at = letter * BASE_ROWS + b * streams + s
                piece = base_ref[s, letter : letter + 1, b * LANES : (b + 1) * LANES]
                base_scr[at : at + 1, :] = piece.astype(jnp.float32)
    first = own * lead_rows
    for half_index, out_ref in enumerate((near_ref, far_ref)):

        def fill(i, carry):
            k = order_ref[half_index * half + i]
            for w in range(own):
                out_ref[i, w * lead_rows : (w + 1) * lead_rows, :] = got_ref[row_ref[k * own + w]]
                at = first + w * BASE_ROWS
                source = pl.multiple_of(allele_ref[k * own + w] * BASE_ROWS, BASE_ROWS)
                piece = base_scr[pl.ds(source, BASE_ROWS), :]
                out_ref[i, at : at + BASE_ROWS, :] = piece.astype(jnp.bfloat16)
            return carry

        lax.fori_loop(0, half, fill, 0)


def pack_of(own, row, allele, order, got, base):
    rows = own * (got.shape[1] + BASE_ROWS)
    half = jax.ShapeDtypeStruct((order.shape[0] // 2, rows, LANES), jnp.bfloat16)
    return pl.pallas_call(
        functools.partial(pack_kernel, own),
        out_shape=(half, half),
        in_specs=[pl.BlockSpec(memory_space=pltpu.SMEM)] * 3 + [pl.BlockSpec(memory_space=pltpu.VMEM)] * 2,
        out_specs=[pl.BlockSpec(memory_space=pltpu.VMEM)] * 2,
        scratch_shapes=[pltpu.VMEM((base.shape[1] * BASE_ROWS, LANES), jnp.float32)],
        compiler_params=pltpu.CompilerParams(vmem_limit_bytes=24 * 2**20),
        name="pack",
    )(row, allele, order, pltpu.with_memory_space_constraint(got, pltpu.VMEM), base)


def mixer_kernel(dims, pos_ref, order_ref, proj_ref, pack_ref, par_ref, gate_ref, part_ref,
                 x_scr, l_scr, p_scr, f_scr, b_scr, m_scr):
    taps, lead_len, groups = dims
    place = order_ref[pl.program_id(0)]
    wins, streams, _, width = proj_ref.shape
    blocks = width // LANES
    rows = wins * blocks
    lead_rows = lead_len * streams
    f32 = jnp.float32
    span = blocks * lead_rows
    first = wins * span
    par_rows = blocks * TAP_ROWS
    spread_row = lax.broadcasted_iota(jnp.int32, (groups, width), 0)
    spread_col = lax.broadcasted_iota(jnp.int32, (groups, width), 1) // (width // groups)
    spread = (spread_row == spread_col).astype(jnp.bfloat16)
    filt = par_ref[0, par_rows : par_rows + groups, :]
    wide = lax.dot_general(filt, spread, (((0,), (0,)), ((), ())), preferred_element_type=f32)
    for w in range(wins):
        l_scr[w * span : (w + 1) * span, :] = pack_ref[0, w * span : (w + 1) * span, :].astype(f32)
        p_scr[w * par_rows : (w + 1) * par_rows, :] = par_ref[0, :par_rows, :].astype(f32)
        at = first + w * BASE_ROWS
        b_scr[w * BASE_ROWS : (w + 1) * BASE_ROWS, :] = pack_ref[0, at : at + BASE_ROWS, :].astype(f32)
        for b in range(blocks):
            q = w * blocks + b
            lanes = slice(b * LANES, (b + 1) * LANES)
            f_scr[q * TIME : (q + 1) * TIME, :] = wide[:TIME, lanes]
            for s in range(streams):
                x_scr[s, q * TIME : (q + 1) * TIME, :] = proj_ref[w, s, :, lanes].astype(f32)
    for w in range(wins):
        for s in range(streams):
            for b in range(blocks):
                q = w * blocks + b
                source = w * BASE_ROWS + b * streams + s
                x_scr[s, pl.ds(q * TIME + pos_ref[w], 1), :] = b_scr[source : source + 1, :]

    def param(r):
        return p_scr[pl.ds(r, rows, stride=TAP_ROWS), :]

    def entry(s, r):
        if r < lead_len:
            return l_scr[pl.ds(r * streams + s, rows, stride=lead_rows), :]
        return x_scr[s, pl.ds(r - lead_len, rows, stride=TIME), :]

    def featured(s):
        weight = [param(s * taps + j) for j in range(taps)]
        window = [entry(s, r) for r in range(taps - 1)]
        for t in range(TIME):
            window.append(entry(s, t + taps - 1))
            total = weight[0] * window[taps - 1]
            for j in range(1, taps):
                total = total + weight[j] * window[taps - 1 - j]
            window.pop(0)
            yield total

    for t, (one, two) in enumerate(zip(featured(1), featured(2))):
        m_scr[t] = (one * two).astype(jnp.bfloat16).astype(f32)
    skip = param(streams * taps)
    for t, gate in enumerate(featured(0)):
        gate_ref[place, pl.ds(t, rows, stride=TIME), :] = gate
    step = 8
    for start in range(0, TIME, step):
        total = [None] * step
        for j in range(start + step):
            tap = f_scr[pl.ds(j, rows, stride=TIME), :]
            for i in range(step):
                at = start + i - j
                if at >= 0:
                    term = tap * m_scr[at]
                    total[i] = term if total[i] is None else total[i] + term
        for i in range(step):
            t = start + i
            part_ref[0, pl.ds(t, rows, stride=TIME), :] = total[i] + skip * m_scr[t]


def mixer_of(dims, position, order, proj, packed, params):
    wins, streams, _, total = proj.shape
    parts = packed.shape[0]
    width = total // parts
    blocks = width // LANES
    rows = wins * blocks
    lead_rows = dims[1] * streams
    shape = pltpu.VMEM((parts, rows * TIME, LANES), jnp.float32)
    late = pltpu.HBM((parts, rows * TIME, LANES), jnp.float32)
    late_spec = pl.BlockSpec((1, rows * TIME, LANES), lambda k, pos, order: (order[k], 0, 0))
    return pl.pallas_call(
        functools.partial(mixer_kernel, dims),
        out_shape=(shape, late),
        grid_spec=pltpu.PrefetchScalarGridSpec(
            num_scalar_prefetch=2,
            grid=(parts,),
            in_specs=[
                pl.BlockSpec((wins, streams, TIME, width), lambda k, pos, order: (0, 0, 0, order[k])),
                pl.BlockSpec((1,) + packed.shape[1:], lambda k, *_: (k, 0, 0)),
                pl.BlockSpec((1,) + params.shape[1:], lambda k, pos, order: (order[k], 0, 0)),
            ],
            out_specs=[pl.BlockSpec(memory_space=pltpu.VMEM), late_spec],
            scratch_shapes=[
                pltpu.VMEM((streams, rows * TIME, LANES), jnp.float32),
                pltpu.VMEM((rows * lead_rows, LANES), jnp.float32),
                pltpu.VMEM((rows * TAP_ROWS, LANES), jnp.float32),
                pltpu.VMEM((rows * TIME, LANES), jnp.float32),
                pltpu.VMEM((wins * BASE_ROWS, LANES), jnp.float32),
                pltpu.VMEM((TIME, rows, LANES), jnp.float32),
            ],
        ),
        compiler_params=pltpu.CompilerParams(vmem_limit_bytes=24 * 2**20),
        cost_estimate=pl.CostEstimate(flops=2 * 10**9, bytes_accessed=10 * 2**20, transcendentals=0),
        name="mixer",
    )(position, order, proj, packed, params)


def combine_kernel(gate_ref, part_ref, carried_ref, out_ref):
    step, rows, _ = part_ref.shape
    wins = out_ref.shape[0]
    blocks = rows // TIME // wins
    first = pl.program_id(0) * step
    for k in range(step):
        for w in range(wins):
            for b in range(blocks):
                at = slice((w * blocks + b) * TIME, (w * blocks + b + 1) * TIME)
                lanes = slice((k * blocks + b) * LANES, (k * blocks + b + 1) * LANES)
                filtered = part_ref[k, at, :] + carried_ref[first + k, at, :].astype(jnp.float32)
                out_ref[w, :, lanes] = (gate_ref[first + k, at, :] * filtered).astype(jnp.bfloat16)


def combine_of(gate, part, carried, wins):
    parts, rows, _ = gate.shape
    width = rows // TIME // wins * LANES
    step = min(4, parts)
    return pl.pallas_call(
        combine_kernel,
        out_shape=jax.ShapeDtypeStruct((wins, TIME, parts * width), jnp.bfloat16),
        grid=(parts // step,),
        in_specs=[
            pl.BlockSpec(memory_space=pltpu.VMEM),
            pl.BlockSpec((step, rows, LANES), lambda k: (k, 0, 0)),
            pl.BlockSpec(memory_space=pltpu.VMEM),
        ],
        out_specs=pl.BlockSpec((wins, TIME, step * width), lambda k: (0, 0, k)),
        compiler_params=pltpu.CompilerParams(vmem_limit_bytes=24 * 2**20),
        name="combine",
    )(gate, pltpu.with_memory_space_constraint(part, pltpu.HBM), pltpu.with_memory_space_constraint(carried, pltpu.VMEM))


def rank_of(keys):
    count = keys.shape[-1]
    same = keys[..., :, None] == keys[..., None, :]
    earlier = jnp.arange(count)[None, :] < jnp.arange(count)[:, None]
    return jnp.sum((same & earlier).astype(jnp.int32), axis=-1)


def slots_of(mask, values, capacity):
    rank = jnp.cumsum(mask.astype(jnp.int32), axis=-1) - 1
    hit = mask[..., None, :] & (rank[..., None, :] == jnp.arange(capacity)[:, None])
    return jnp.sum(jnp.where(hit, values[..., None, :], 0), axis=-1)


def take_rows(array, index):
    return array.at[index].get(mode="promise_in_bounds")


def local(
    projected,
    cache_history,
    cache_inputs,
    feature_taps,
    filters,
    skip_weight,
    base_inputs,
    window_owner,
    window_slot,
    variant_position,
    allele,
):
    var_count, tp_count = lax.axis_size("var"), lax.axis_size("tp")
    me, part = lax.axis_index("var"), lax.axis_index("tp")
    windows, own = variant_position.shape[0], projected.shape[0]
    loci, _, width = cache_history.shape
    group_size = width // filters.shape[1]
    taps, streams = feature_taps.shape[:2]
    lead_len = cache_inputs.shape[1]
    filters_t = filters.T

    owners = window_owner.reshape(var_count, windows)
    slots = window_slot.reshape(var_count, windows)
    pick = slots_of(owners == me, slots, CAPACITY).reshape(-1)
    own_owner = lax.dynamic_index_in_dim(owners, me, 0, keepdims=False)
    own_row = own_owner * CAPACITY + rank_of(own_owner)

    def exchange(rows):
        got = lax.all_to_all(rows.reshape(var_count, -1, LANES), "var", split_axis=0, concat_axis=0, tiled=True)
        return got.reshape(rows.shape)

    lead = exchange(lead_of(me, window_owner, window_slot, cache_inputs, windows))
    carried = take_rows(owner_of(cache_history, filters_t, group_size), pick)
    params = params_of(feature_taps.transpose(1, 0, 2), skip_weight[None], filters_t)
    params = lax.all_gather(params, "tp", axis=0)
    carried, lead, params = lax.optimization_barrier((carried, lead, params))
    carried = exchange(carried)

    half = tp_count // 2
    line, core = part // 2, part % 2
    steps = jnp.arange(half)
    targets = (line + steps) % half * 2
    near, far = pack_of(
        own,
        own_row,
        allele,
        jnp.concatenate([targets + core, targets + 1 - core]),
        lead,
        base_inputs.transpose(1, 0, 2),
    )
    other = lax.ppermute(far, "tp", [(k, k ^ 1) for k in range(tp_count)])
    both = [jnp.stack([near[step], other[step]]) for step in range(half)]
    for step in sorted(range(1, half), key=lambda step: -min(step, half - step)):
        both[step] = lax.ppermute(both[step], "tp", [(k, (k + 2 * step) % tp_count) for k in range(tp_count)])
    packed = jnp.concatenate(both, axis=0)
    sources = (line - steps) % half * 2
    order = jnp.stack([sources + core, sources + 1 - core], axis=1).reshape(-1)

    carried, _ = lax.optimization_barrier((carried, packed))
    carried = take_rows(carried, own_row).reshape(tp_count, -1, LANES)
    carried = lax.all_to_all(carried, "tp", split_axis=0, concat_axis=0, tiled=True)

    position = lax.dynamic_slice(variant_position, (part * own,), (own,))
    gate, partial = mixer_of(
        (taps, lead_len, filters_t.shape[0]), position, order, projected.transpose(0, 2, 1, 3), packed, params
    )
    return combine_of(gate, partial, carried, own)


def solution(mesh):
    return jax.shard_map(
        local,
        mesh=mesh,
        in_specs=(
            P(("var", "tp"), None, None, None),
            P("var", None, "tp"),
            P("var", None, None, "tp"),
            P(None, None, "tp"),
            P(None, "tp"),
            P("tp"),
            P(None, None, "tp"),
            P(),
            P(),
            P("var"),
            P("var"),
        ),
        out_specs=P(("var", "tp"), None, None),
        check_vma=False,
    )
```

```python
import functools
import jax
import jax.numpy as jnp
from jax import lax
from jax.experimental import pallas as pl
from jax.experimental.pallas import tpu as pltpu
from jax.sharding import PartitionSpec as P

LANES = 128
TAP_ROWS = 24
BASE_ROWS = 16
CAPACITY = 2
TIME = 32


def lead_kernel(windows, me_ref, owner_ref, slot_ref, inputs_ref, send_ref, rows_scr):
    loci, lead_len, streams, width = inputs_ref.shape
    blocks = width // LANES
    f32 = jnp.float32
    for n in range(loci):
        for r in range(lead_len):
            for b in range(blocks):
                at = ((n * blocks + b) * lead_len + r) * streams
                piece = inputs_ref[n, r, :, b * LANES : (b + 1) * LANES]
                rows_scr[at : at + streams, :] = piece.astype(f32)
    lanes = owner_ref.shape[1]
    row = lax.broadcasted_iota(jnp.int32, (lanes, lanes), 0)
    col = lax.broadcasted_iota(jnp.int32, (lanes, lanes), 1)
    before = ((row // windows == col // windows) & (row < col)).astype(jnp.bfloat16)
    gather = (row // windows == col).astype(jnp.bfloat16)
    mine = owner_ref[...] == me_ref[0]
    rank = jnp.dot(mine.astype(f32).astype(jnp.bfloat16), before, preferred_element_type=f32)
    slot = slot_ref[...].astype(f32)
    span = blocks * lead_len * streams
    segments = lanes // windows
    picks = []
    for r in range(CAPACITY):
        value = jnp.where(mine & (rank == r), slot, 0.0).astype(jnp.bfloat16)
        picks.append(jnp.dot(value, gather, preferred_element_type=f32))
    for i in range(send_ref.shape[0]):
        target, r = i // CAPACITY, i % CAPACITY
        pick = picks[r][target // segments : target // segments + 1, target % segments : target % segments + 1]
        pick = jnp.broadcast_to(pick, (span, LANES))
        found = rows_scr[:span, :]
        for n in range(1, loci):
            found = jnp.where(pick == n, rows_scr[n * span : (n + 1) * span, :], found)
        send_ref[i] = found.astype(jnp.bfloat16)


def lead_of(me, owners, slots, inputs, windows):
    loci, lead_len, streams, width = inputs.shape
    rows = width // LANES * lead_len * streams
    targets = slots.shape[0] // windows
    lanes = min(LANES, slots.shape[0])
    return pl.pallas_call(
        functools.partial(lead_kernel, windows),
        out_shape=jax.ShapeDtypeStruct((targets * CAPACITY, rows, LANES), jnp.bfloat16),
        in_specs=[pl.BlockSpec(memory_space=pltpu.SMEM)] + [pl.BlockSpec(memory_space=pltpu.VMEM)] * 3,
        out_specs=pl.BlockSpec(memory_space=pltpu.VMEM),
        scratch_shapes=[pltpu.VMEM((loci * rows, LANES), jnp.float32)],
        name="lead",
    )(me.reshape(1), owners.reshape(-1, lanes), slots.reshape(-1, lanes), inputs)


def owner_kernel(group_size, history_ref, filters_ref, carried_ref, line_scr):
    loci, history_len, width = history_ref.shape
    tap_count = filters_ref.shape[1]
    blocks = width // LANES
    per_block = LANES // group_size
    f32 = jnp.float32
    row = lax.broadcasted_iota(jnp.int32, (tap_count, tap_count), 0)
    col = lax.broadcasted_iota(jnp.int32, (tap_count, tap_count), 1)
    flip = (row + col == tap_count - 1).astype(jnp.bfloat16)
    line_scr[...] = jnp.dot(filters_ref[...], flip, preferred_element_type=f32)
    t_row = lax.broadcasted_iota(jnp.int32, (TIME, tap_count), 0)
    s_col = lax.broadcasted_iota(jnp.int32, (TIME, tap_count), 1)
    valid = (s_col >= t_row) & (s_col < history_len)
    lane = lax.broadcasted_iota(jnp.int32, (TIME, LANES), 1) // group_size
    for b in range(blocks):
        tables = []
        for g in range(per_block):
            index = b * per_block + g
            line = jnp.broadcast_to(line_scr[index : index + 1, :], (TIME, tap_count))
            turned = pltpu.roll(line, 0, 1, stride=1, stride_axis=0)
            tables.append(jnp.where(valid, turned, 0.0))
        table = jnp.concatenate(tables, axis=0).astype(jnp.bfloat16)[:, :history_len]
        for n in range(loci):
            past = history_ref[n, :, b * LANES : (b + 1) * LANES]
            full = jnp.dot(table, past, preferred_element_type=f32)
            total = jnp.zeros((TIME, LANES), f32)
            for g in range(per_block):
                total = jnp.where(lane == g, full[g * TIME : (g + 1) * TIME], total)
            carried_ref[n, b * TIME : (b + 1) * TIME, :] = total.astype(jnp.bfloat16)


def owner_of(history, filters_t, group_size):
    loci, _, width = history.shape
    return pl.pallas_call(
        functools.partial(owner_kernel, group_size),
        out_shape=jax.ShapeDtypeStruct((loci, width // LANES * TIME, LANES), jnp.bfloat16),
        in_specs=[pl.BlockSpec(memory_space=pltpu.VMEM)] * 2,
        out_specs=pl.BlockSpec(memory_space=pltpu.VMEM),
        scratch_shapes=[pltpu.VMEM(filters_t.shape, jnp.float32)],
        name="owner",
    )(history, filters_t)


def params_kernel(taps_ref, skip_ref, filters_ref, out_ref, par_scr):
    streams, taps, width = taps_ref.shape
    f32 = jnp.float32
    par_scr[...] = jnp.zeros_like(par_scr)
    for b in range(width // LANES):
        lanes = slice(b * LANES, (b + 1) * LANES)
        for s in range(streams):
            at = b * TAP_ROWS + s * taps
            par_scr[at : at + taps, :] = taps_ref[s, :, lanes].astype(f32)
        at = b * TAP_ROWS + streams * taps
        par_scr[at : at + 1, :] = skip_ref[:, lanes].astype(f32)
    rows = par_scr.shape[0]
    out_ref[:rows, :] = par_scr[...].astype(jnp.bfloat16)
    out_ref[rows:, :] = filters_ref[...]


def params_of(taps, skip, filters_t):
    rows = taps.shape[2] // LANES * TAP_ROWS
    return pl.pallas_call(
        params_kernel,
        out_shape=jax.ShapeDtypeStruct((rows + filters_t.shape[0], LANES), jnp.bfloat16),
        in_specs=[pl.BlockSpec(memory_space=pltpu.VMEM)] * 3,
        out_specs=pl.BlockSpec(memory_space=pltpu.VMEM),
        scratch_shapes=[pltpu.VMEM((rows, LANES), jnp.float32)],
        name="params",
    )(taps, skip, filters_t)


def pack_kernel(own, row_ref, allele_ref, order_ref, got_ref, base_ref, params_ref, near_ref, far_ref, base_scr):
    half = near_ref.shape[0]
    lead_rows = got_ref.shape[1]
    streams, bases, width = base_ref.shape
    base_scr[...] = jnp.zeros_like(base_scr)
    for b in range(width // LANES):
        for s in range(streams):
            for letter in range(bases):
                at = letter * BASE_ROWS + b * streams + s
                piece = base_ref[s, letter : letter + 1, b * LANES : (b + 1) * LANES]
                base_scr[at : at + 1, :] = piece.astype(jnp.float32)
    first = own * lead_rows
    for half_index, out_ref in enumerate((near_ref, far_ref)):

        def fill(i, carry):
            k = order_ref[half_index * half + i]
            out_ref[i, first + own * BASE_ROWS :, :] = params_ref[...]
            for w in range(own):
                out_ref[i, w * lead_rows : (w + 1) * lead_rows, :] = got_ref[row_ref[k * own + w]]
                at = first + w * BASE_ROWS
                source = pl.multiple_of(allele_ref[k * own + w] * BASE_ROWS, BASE_ROWS)
                piece = base_scr[pl.ds(source, BASE_ROWS), :]
                out_ref[i, at : at + BASE_ROWS, :] = piece.astype(jnp.bfloat16)
            return carry

        lax.fori_loop(0, half, fill, 0)


def pack_of(own, row, allele, order, got, base, params):
    rows = own * (got.shape[1] + BASE_ROWS) + params.shape[0]
    half = jax.ShapeDtypeStruct((order.shape[0] // 2, rows, LANES), jnp.bfloat16)
    return pl.pallas_call(
        functools.partial(pack_kernel, own),
        out_shape=(half, half),
        in_specs=[pl.BlockSpec(memory_space=pltpu.SMEM)] * 3 + [pl.BlockSpec(memory_space=pltpu.VMEM)] * 3,
        out_specs=[pl.BlockSpec(memory_space=pltpu.VMEM)] * 2,
        scratch_shapes=[pltpu.VMEM((base.shape[1] * BASE_ROWS, LANES), jnp.float32)],
        compiler_params=pltpu.CompilerParams(vmem_limit_bytes=24 * 2**20),
        name="pack",
    )(row, allele, order, pltpu.with_memory_space_constraint(got, pltpu.VMEM), base, params)


def mixer_kernel(dims, pos_ref, order_ref, proj_ref, pack_ref, gate_ref, part_ref,
                 x_scr, l_scr, p_scr, f_scr, b_scr, m_scr):
    taps, lead_len, groups = dims
    place = order_ref[pl.program_id(0)]
    wins, streams, _, width = proj_ref.shape
    blocks = width // LANES
    rows = wins * blocks
    lead_rows = lead_len * streams
    f32 = jnp.float32
    span = blocks * lead_rows
    first = wins * span
    par_rows = blocks * TAP_ROWS
    shared = first + wins * BASE_ROWS
    spread_row = lax.broadcasted_iota(jnp.int32, (groups, width), 0)
    spread_col = lax.broadcasted_iota(jnp.int32, (groups, width), 1) // (width // groups)
    spread = (spread_row == spread_col).astype(jnp.bfloat16)
    filt = pack_ref[0, shared + par_rows : shared + par_rows + groups, :]
    wide = lax.dot_general(filt, spread, (((0,), (0,)), ((), ())), preferred_element_type=f32)
    for w in range(wins):
        l_scr[w * span : (w + 1) * span, :] = pack_ref[0, w * span : (w + 1) * span, :].astype(f32)
        p_scr[w * par_rows : (w + 1) * par_rows, :] = pack_ref[0, shared : shared + par_rows, :].astype(f32)
        at = first + w * BASE_ROWS
        b_scr[w * BASE_ROWS : (w + 1) * BASE_ROWS, :] = pack_ref[0, at : at + BASE_ROWS, :].astype(f32)
        for b in range(blocks):
            q = w * blocks + b
            lanes = slice(b * LANES, (b + 1) * LANES)
            f_scr[q * TIME : (q + 1) * TIME, :] = wide[:TIME, lanes]
            for s in range(streams):
                x_scr[s, q * TIME : (q + 1) * TIME, :] = proj_ref[w, s, :, lanes].astype(f32)
    for w in range(wins):
        for s in range(streams):
            for b in range(blocks):
                q = w * blocks + b
                source = w * BASE_ROWS + b * streams + s
                x_scr[s, pl.ds(q * TIME + pos_ref[w], 1), :] = b_scr[source : source + 1, :]

    def param(r):
        return p_scr[pl.ds(r, rows, stride=TAP_ROWS), :]

    def entry(s, r):
        if r < lead_len:
            return l_scr[pl.ds(r * streams + s, rows, stride=lead_rows), :]
        return x_scr[s, pl.ds(r - lead_len, rows, stride=TIME), :]

    def featured(s):
        weight = [param(s * taps + j) for j in range(taps)]
        window = [entry(s, r) for r in range(taps - 1)]
        for t in range(TIME):
            window.append(entry(s, t + taps - 1))
            total = weight[0] * window[taps - 1]
            for j in range(1, taps):
                total = total + weight[j] * window[taps - 1 - j]
            window.pop(0)
            yield total

    for t, (one, two) in enumerate(zip(featured(1), featured(2))):
        m_scr[t] = (one * two).astype(jnp.bfloat16).astype(f32)
    skip = param(streams * taps)
    for t, gate in enumerate(featured(0)):
        gate_ref[place, pl.ds(t, rows, stride=TIME), :] = gate
    step = 8
    for start in range(0, TIME, step):
        total = [None] * step
        for j in range(start + step):
            tap = f_scr[pl.ds(j, rows, stride=TIME), :]
            for i in range(step):
                at = start + i - j
                if at >= 0:
                    term = tap * m_scr[at]
                    total[i] = term if total[i] is None else total[i] + term
        for i in range(step):
            t = start + i
            part_ref[0, pl.ds(t, rows, stride=TIME), :] = total[i] + skip * m_scr[t]


def mixer_of(dims, position, order, proj, packed):
    wins, streams, _, total = proj.shape
    parts = packed.shape[0]
    width = total // parts
    blocks = width // LANES
    rows = wins * blocks
    lead_rows = dims[1] * streams
    shape = pltpu.VMEM((parts, rows * TIME, LANES), jnp.float32)
    late = pltpu.HBM((parts, rows * TIME, LANES), jnp.float32)
    late_spec = pl.BlockSpec((1, rows * TIME, LANES), lambda k, pos, order: (order[k], 0, 0))
    return pl.pallas_call(
        functools.partial(mixer_kernel, dims),
        out_shape=(shape, late),
        grid_spec=pltpu.PrefetchScalarGridSpec(
            num_scalar_prefetch=2,
            grid=(parts,),
            in_specs=[
                pl.BlockSpec((wins, streams, TIME, width), lambda k, pos, order: (0, 0, 0, order[k])),
                pl.BlockSpec((1,) + packed.shape[1:], lambda k, *_: (k, 0, 0)),
            ],
            out_specs=[pl.BlockSpec(memory_space=pltpu.VMEM), late_spec],
            scratch_shapes=[
                pltpu.VMEM((streams, rows * TIME, LANES), jnp.float32),
                pltpu.VMEM((rows * lead_rows, LANES), jnp.float32),
                pltpu.VMEM((rows * TAP_ROWS, LANES), jnp.float32),
                pltpu.VMEM((rows * TIME, LANES), jnp.float32),
                pltpu.VMEM((wins * BASE_ROWS, LANES), jnp.float32),
                pltpu.VMEM((TIME, rows, LANES), jnp.float32),
            ],
        ),
        compiler_params=pltpu.CompilerParams(vmem_limit_bytes=24 * 2**20),
        cost_estimate=pl.CostEstimate(flops=2 * 10**9, bytes_accessed=10 * 2**20, transcendentals=0),
        name="mixer",
    )(position, order, proj, packed)


def combine_kernel(gate_ref, part_hbm, carried_ref, out_ref, part_ref, sem):
    parts, rows, _ = gate_ref.shape
    wins, _, total = out_ref.shape
    blocks = rows // TIME // wins
    width = total // parts
    count = sem.shape[0]
    step = parts // count
    copies = []
    for c in range(count):
        span = pl.ds(c * step, step)
        copies.append(pltpu.make_async_copy(part_hbm.at[span], part_ref.at[span], sem.at[c]))
        copies[-1].start()
    for c in range(count):
        copies[c].wait()

        def body(i, carry):
            k = c * step + i
            for w in range(wins):
                for b in range(blocks):
                    at = slice((w * blocks + b) * TIME, (w * blocks + b + 1) * TIME)
                    lanes = pl.ds(pl.multiple_of(k * width + b * LANES, LANES), LANES)
                    filtered = part_ref[k, at, :] + carried_ref[k, at, :].astype(jnp.float32)
                    out_ref[w, :, lanes] = (gate_ref[k, at, :] * filtered).astype(jnp.bfloat16)
            return carry

        lax.fori_loop(0, step, body, 0)


def combine_of(gate, part, carried, wins):
    parts, rows, _ = gate.shape
    width = rows // TIME // wins * LANES
    return pl.pallas_call(
        combine_kernel,
        out_shape=jax.ShapeDtypeStruct((wins, TIME, parts * width), jnp.bfloat16),
        in_specs=[
            pl.BlockSpec(memory_space=pltpu.VMEM),
            pl.BlockSpec(memory_space=pltpu.HBM),
            pl.BlockSpec(memory_space=pltpu.VMEM),
        ],
        out_specs=pl.BlockSpec(memory_space=pltpu.VMEM),
        scratch_shapes=[pltpu.VMEM(part.shape, jnp.float32), pltpu.SemaphoreType.DMA((4,))],
        compiler_params=pltpu.CompilerParams(vmem_limit_bytes=24 * 2**20),
        name="combine",
    )(gate, pltpu.with_memory_space_constraint(part, pltpu.HBM), pltpu.with_memory_space_constraint(carried, pltpu.VMEM))


def rank_of(keys):
    count = keys.shape[-1]
    same = keys[..., :, None] == keys[..., None, :]
    earlier = jnp.arange(count)[None, :] < jnp.arange(count)[:, None]
    return jnp.sum((same & earlier).astype(jnp.int32), axis=-1)


def slots_of(mask, values, capacity):
    rank = jnp.cumsum(mask.astype(jnp.int32), axis=-1) - 1
    hit = mask[..., None, :] & (rank[..., None, :] == jnp.arange(capacity)[:, None])
    return jnp.sum(jnp.where(hit, values[..., None, :], 0), axis=-1)


def take_rows(array, index):
    return array.at[index].get(mode="promise_in_bounds")


def local(
    projected,
    cache_history,
    cache_inputs,
    feature_taps,
    filters,
    skip_weight,
    base_inputs,
    window_owner,
    window_slot,
    variant_position,
    allele,
):
    var_count, tp_count = lax.axis_size("var"), lax.axis_size("tp")
    me, part = lax.axis_index("var"), lax.axis_index("tp")
    windows, own = variant_position.shape[0], projected.shape[0]
    loci, _, width = cache_history.shape
    group_size = width // filters.shape[1]
    taps, streams = feature_taps.shape[:2]
    lead_len = cache_inputs.shape[1]
    filters_t = filters.T

    owners = window_owner.reshape(var_count, windows)
    slots = window_slot.reshape(var_count, windows)
    pick = slots_of(owners == me, slots, CAPACITY).reshape(-1)
    own_owner = lax.dynamic_index_in_dim(owners, me, 0, keepdims=False)
    own_row = own_owner * CAPACITY + rank_of(own_owner)

    def exchange(rows):
        got = lax.all_to_all(rows.reshape(var_count, -1, LANES), "var", split_axis=0, concat_axis=0, tiled=True)
        return got.reshape(rows.shape)

    lead = exchange(lead_of(me, window_owner, window_slot, cache_inputs, windows))
    carried = take_rows(owner_of(cache_history, filters_t, group_size), pick)
    params = params_of(feature_taps.transpose(1, 0, 2), skip_weight[None], filters_t)
    carried, lead, params = lax.optimization_barrier((carried, lead, params))
    carried = exchange(carried)

    half = tp_count // 2
    line, core = part // 2, part % 2
    steps = jnp.arange(half)
    targets = (line + steps) % half * 2
    near, far = pack_of(
        own,
        own_row,
        allele,
        jnp.concatenate([targets + core, targets + 1 - core]),
        lead,
        base_inputs.transpose(1, 0, 2),
        params,
    )
    other = lax.ppermute(far, "tp", [(k, k ^ 1) for k in range(tp_count)])
    both = [jnp.stack([near[step], other[step]]) for step in range(half)]
    for step in sorted(range(1, half), key=lambda step: -min(step, half - step)):
        both[step] = lax.ppermute(both[step], "tp", [(k, (k + 2 * step) % tp_count) for k in range(tp_count)])
    packed = jnp.concatenate(both, axis=0)
    sources = (line - steps) % half * 2
    order = jnp.stack([sources + core, sources + 1 - core], axis=1).reshape(-1)

    carried, _ = lax.optimization_barrier((carried, packed))
    carried = take_rows(carried, own_row).reshape(tp_count, -1, LANES)
    carried = lax.all_to_all(carried, "tp", split_axis=0, concat_axis=0, tiled=True)

    position = lax.dynamic_slice(variant_position, (part * own,), (own,))
    gate, partial = mixer_of(
        (taps, lead_len, filters_t.shape[0]), position, order, projected.transpose(0, 2, 1, 3), packed
    )
    return combine_of(gate, partial, carried, own)


def solution(mesh):
    return jax.shard_map(
        local,
        mesh=mesh,
        in_specs=(
            P(("var", "tp"), None, None, None),
            P("var", None, "tp"),
            P("var", None, None, "tp"),
            P(None, None, "tp"),
            P(None, "tp"),
            P("tp"),
            P(None, None, "tp"),
            P(),
            P(),
            P("var"),
            P("var"),
        ),
        out_specs=P(("var", "tp"), None, None),
        check_vma=False,
    )
```

```python
import functools
import jax
import jax.numpy as jnp
from jax import lax
from jax.experimental import pallas as pl
from jax.experimental.pallas import tpu as pltpu
from jax.sharding import PartitionSpec as P

LANES = 128
TAP_ROWS = 22
BASE_ROWS = 16
CAPACITY = 2
TIME = 32


def lead_kernel(windows, me_ref, owner_ref, slot_ref, inputs_ref, send_ref, rows_scr):
    loci, lead_len, streams, width = inputs_ref.shape
    blocks = width // LANES
    f32 = jnp.float32
    for n in range(loci):
        for r in range(lead_len):
            for b in range(blocks):
                at = ((n * blocks + b) * lead_len + r) * streams
                piece = inputs_ref[n, r, :, b * LANES : (b + 1) * LANES]
                rows_scr[at : at + streams, :] = piece.astype(f32)
    lanes = owner_ref.shape[1]
    row = lax.broadcasted_iota(jnp.int32, (lanes, lanes), 0)
    col = lax.broadcasted_iota(jnp.int32, (lanes, lanes), 1)
    before = ((row // windows == col // windows) & (row < col)).astype(jnp.bfloat16)
    gather = (row // windows == col).astype(jnp.bfloat16)
    mine = owner_ref[...] == me_ref[0]
    rank = jnp.dot(mine.astype(f32).astype(jnp.bfloat16), before, preferred_element_type=f32)
    slot = slot_ref[...].astype(f32)
    span = blocks * lead_len * streams
    segments = lanes // windows
    picks = []
    for r in range(CAPACITY):
        value = jnp.where(mine & (rank == r), slot, 0.0).astype(jnp.bfloat16)
        picks.append(jnp.dot(value, gather, preferred_element_type=f32))
    for i in range(send_ref.shape[0]):
        target, r = i // CAPACITY, i % CAPACITY
        pick = picks[r][target // segments : target // segments + 1, target % segments : target % segments + 1]
        pick = jnp.broadcast_to(pick, (span, LANES))
        found = rows_scr[:span, :]
        for n in range(1, loci):
            found = jnp.where(pick == n, rows_scr[n * span : (n + 1) * span, :], found)
        send_ref[i] = found.astype(jnp.bfloat16)


def lead_of(me, owners, slots, inputs, windows):
    loci, lead_len, streams, width = inputs.shape
    rows = width // LANES * lead_len * streams
    targets = slots.shape[0] // windows
    lanes = min(LANES, slots.shape[0])
    return pl.pallas_call(
        functools.partial(lead_kernel, windows),
        out_shape=jax.ShapeDtypeStruct((targets * CAPACITY, rows, LANES), jnp.bfloat16),
        in_specs=[pl.BlockSpec(memory_space=pltpu.SMEM)] + [pl.BlockSpec(memory_space=pltpu.VMEM)] * 3,
        out_specs=pl.BlockSpec(memory_space=pltpu.VMEM),
        scratch_shapes=[pltpu.VMEM((loci * rows, LANES), jnp.float32)],
        name="lead",
    )(me.reshape(1), owners.reshape(-1, lanes), slots.reshape(-1, lanes), inputs)


def owner_kernel(group_size, history_ref, filters_ref, carried_ref, line_scr):
    loci, history_len, width = history_ref.shape
    tap_count = filters_ref.shape[1]
    blocks = width // LANES
    per_block = LANES // group_size
    f32 = jnp.float32
    row = lax.broadcasted_iota(jnp.int32, (tap_count, tap_count), 0)
    col = lax.broadcasted_iota(jnp.int32, (tap_count, tap_count), 1)
    flip = (row + col == tap_count - 1).astype(jnp.bfloat16)
    line_scr[...] = jnp.dot(filters_ref[...], flip, preferred_element_type=f32)
    t_row = lax.broadcasted_iota(jnp.int32, (TIME, tap_count), 0)
    s_col = lax.broadcasted_iota(jnp.int32, (TIME, tap_count), 1)
    valid = (s_col >= t_row) & (s_col < history_len)
    lane = lax.broadcasted_iota(jnp.int32, (TIME, LANES), 1) // group_size
    for b in range(blocks):
        tables = []
        for g in range(per_block):
            index = b * per_block + g
            line = jnp.broadcast_to(line_scr[index : index + 1, :], (TIME, tap_count))
            turned = pltpu.roll(line, 0, 1, stride=1, stride_axis=0)
            tables.append(jnp.where(valid, turned, 0.0))
        table = jnp.concatenate(tables, axis=0).astype(jnp.bfloat16)[:, :history_len]
        for n in range(loci):
            past = history_ref[n, :, b * LANES : (b + 1) * LANES]
            full = jnp.dot(table, past, preferred_element_type=f32)
            total = jnp.zeros((TIME, LANES), f32)
            for g in range(per_block):
                total = jnp.where(lane == g, full[g * TIME : (g + 1) * TIME], total)
            carried_ref[n, b * TIME : (b + 1) * TIME, :] = total.astype(jnp.bfloat16)


def owner_of(history, filters_t, group_size):
    loci, _, width = history.shape
    return pl.pallas_call(
        functools.partial(owner_kernel, group_size),
        out_shape=jax.ShapeDtypeStruct((loci, width // LANES * TIME, LANES), jnp.bfloat16),
        in_specs=[pl.BlockSpec(memory_space=pltpu.VMEM)] * 2,
        out_specs=pl.BlockSpec(memory_space=pltpu.VMEM),
        scratch_shapes=[pltpu.VMEM(filters_t.shape, jnp.float32)],
        name="owner",
    )(history, filters_t)


def params_kernel(taps_ref, skip_ref, filters_ref, out_ref, par_scr, filt_scr):
    streams, taps, width = taps_ref.shape
    f32 = jnp.float32
    par_scr[...] = jnp.zeros_like(par_scr)
    for b in range(width // LANES):
        lanes = slice(b * LANES, (b + 1) * LANES)
        for s in range(streams):
            at = b * TAP_ROWS + s * taps
            par_scr[at : at + taps, :] = taps_ref[s, :, lanes].astype(f32)
        at = b * TAP_ROWS + streams * taps
        par_scr[at : at + 1, :] = skip_ref[:, lanes].astype(f32)
    rows = par_scr.shape[0]
    out_ref[:rows, :] = par_scr[...].astype(jnp.bfloat16)
    filt_scr[...] = filters_ref[...].astype(f32)
    share = LANES // TIME
    lines = filters_ref.shape[0] // share
    lane = lax.broadcasted_iota(jnp.int32, (lines, LANES), 1) // TIME
    packed = jnp.zeros((lines, LANES), f32)
    for m in range(share):
        line = filt_scr[pl.ds(m, lines, stride=share), :]
        line = pltpu.roll(line, m * TIME, 1) if m else line
        packed = jnp.where(lane == m, line, packed)
    out_ref[rows:, :] = packed.astype(jnp.bfloat16)


def params_of(taps, skip, filters_t):
    rows = taps.shape[2] // LANES * TAP_ROWS
    return pl.pallas_call(
        params_kernel,
        out_shape=jax.ShapeDtypeStruct((rows + filters_t.shape[0] * TIME // LANES, LANES), jnp.bfloat16),
        in_specs=[pl.BlockSpec(memory_space=pltpu.VMEM)] * 3,
        out_specs=pl.BlockSpec(memory_space=pltpu.VMEM),
        scratch_shapes=[pltpu.VMEM((rows, LANES), jnp.float32), pltpu.VMEM(filters_t.shape, jnp.float32)],
        name="params",
    )(taps, skip, filters_t)


def pack_kernel(own, row_ref, allele_ref, order_ref, got_ref, base_ref, params_ref, near_ref, far_ref, base_scr):
    half = near_ref.shape[0]
    lead_rows = got_ref.shape[1]
    streams, bases, width = base_ref.shape
    base_scr[...] = jnp.zeros_like(base_scr)
    for b in range(width // LANES):
        for s in range(streams):
            for letter in range(bases):
                at = letter * BASE_ROWS + b * streams + s
                piece = base_ref[s, letter : letter + 1, b * LANES : (b + 1) * LANES]
                base_scr[at : at + 1, :] = piece.astype(jnp.float32)
    first = own * lead_rows
    for half_index, out_ref in enumerate((near_ref, far_ref)):

        def fill(i, carry):
            k = order_ref[half_index * half + i]
            out_ref[i, first + own * BASE_ROWS :, :] = params_ref[...]
            for w in range(own):
                out_ref[i, w * lead_rows : (w + 1) * lead_rows, :] = got_ref[row_ref[k * own + w]]
                at = first + w * BASE_ROWS
                source = pl.multiple_of(allele_ref[k * own + w] * BASE_ROWS, BASE_ROWS)
                piece = base_scr[pl.ds(source, BASE_ROWS), :]
                out_ref[i, at : at + BASE_ROWS, :] = piece.astype(jnp.bfloat16)
            return carry

        lax.fori_loop(0, half, fill, 0)


def pack_of(own, row, allele, order, got, base, params):
    rows = own * (got.shape[1] + BASE_ROWS) + params.shape[0]
    half = jax.ShapeDtypeStruct((order.shape[0] // 2, rows, LANES), jnp.bfloat16)
    return pl.pallas_call(
        functools.partial(pack_kernel, own),
        out_shape=(half, half),
        in_specs=[pl.BlockSpec(memory_space=pltpu.SMEM)] * 3 + [pl.BlockSpec(memory_space=pltpu.VMEM)] * 3,
        out_specs=[pl.BlockSpec(memory_space=pltpu.VMEM)] * 2,
        scratch_shapes=[pltpu.VMEM((base.shape[1] * BASE_ROWS, LANES), jnp.float32)],
        compiler_params=pltpu.CompilerParams(vmem_limit_bytes=24 * 2**20),
        name="pack",
    )(row, allele, order, pltpu.with_memory_space_constraint(got, pltpu.VMEM), base, params)


def mixer_kernel(dims, pos_ref, order_ref, proj_ref, pack_ref, gate_ref, part_ref,
                 x_scr, l_scr, p_scr, f_scr, b_scr, m_scr):
    taps, lead_len, groups = dims
    place = order_ref[pl.program_id(0)]
    wins, streams, _, width = proj_ref.shape
    blocks = width // LANES
    rows = wins * blocks
    lead_rows = lead_len * streams
    f32 = jnp.float32
    span = blocks * lead_rows
    first = wins * span
    par_rows = blocks * TAP_ROWS
    shared = first + wins * BASE_ROWS
    share = LANES // TIME
    lines = groups // share
    filt = pack_ref[0, shared + par_rows : shared + par_rows + lines, :]
    line = lax.broadcasted_iota(jnp.int32, (lines, width), 0) * share
    group = lax.broadcasted_iota(jnp.int32, (lines, width), 1) // (width // groups)
    wide = jnp.zeros((TIME, width), f32)
    for m in range(share):
        spread = (line + m == group).astype(jnp.bfloat16)
        part = filt[:, m * TIME : (m + 1) * TIME]
        wide += lax.dot_general(part, spread, (((0,), (0,)), ((), ())), preferred_element_type=f32)
    for w in range(wins):
        l_scr[w * span : (w + 1) * span, :] = pack_ref[0, w * span : (w + 1) * span, :].astype(f32)
        p_scr[w * par_rows : (w + 1) * par_rows, :] = pack_ref[0, shared : shared + par_rows, :].astype(f32)
        at = first + w * BASE_ROWS
        b_scr[w * BASE_ROWS : (w + 1) * BASE_ROWS, :] = pack_ref[0, at : at + BASE_ROWS, :].astype(f32)
        for b in range(blocks):
            q = w * blocks + b
            lanes = slice(b * LANES, (b + 1) * LANES)
            f_scr[q * TIME : (q + 1) * TIME, :] = wide[:, lanes]
            for s in range(streams):
                x_scr[s, q * TIME : (q + 1) * TIME, :] = proj_ref[w, s, :, lanes].astype(f32)
    for w in range(wins):
        for s in range(streams):
            for b in range(blocks):
                q = w * blocks + b
                source = w * BASE_ROWS + b * streams + s
                x_scr[s, pl.ds(q * TIME + pos_ref[w], 1), :] = b_scr[source : source + 1, :]

    def param(r):
        return p_scr[pl.ds(r, rows, stride=TAP_ROWS), :]

    def entry(s, r):
        if r < lead_len:
            return l_scr[pl.ds(r * streams + s, rows, stride=lead_rows), :]
        return x_scr[s, pl.ds(r - lead_len, rows, stride=TIME), :]

    def featured(s):
        weight = [param(s * taps + j) for j in range(taps)]
        window = [entry(s, r) for r in range(taps - 1)]
        for t in range(TIME):
            window.append(entry(s, t + taps - 1))
            total = weight[0] * window[taps - 1]
            for j in range(1, taps):
                total = total + weight[j] * window[taps - 1 - j]
            window.pop(0)
            yield total

    for t, (one, two) in enumerate(zip(featured(1), featured(2))):
        m_scr[t] = (one * two).astype(jnp.bfloat16).astype(f32)
    skip = param(streams * taps)
    for t, gate in enumerate(featured(0)):
        gate_ref[place, pl.ds(t, rows, stride=TIME), :] = gate
    step = 8
    for start in range(0, TIME, step):
        total = [None] * step
        for j in range(start + step):
            tap = f_scr[pl.ds(j, rows, stride=TIME), :]
            for i in range(step):
                at = start + i - j
                if at >= 0:
                    term = tap * m_scr[at]
                    total[i] = term if total[i] is None else total[i] + term
        for i in range(step):
            t = start + i
            part_ref[0, pl.ds(t, rows, stride=TIME), :] = total[i] + skip * m_scr[t]


def mixer_of(dims, position, order, proj, packed):
    wins, streams, _, total = proj.shape
    parts = packed.shape[0]
    width = total // parts
    blocks = width // LANES
    rows = wins * blocks
    lead_rows = dims[1] * streams
    shape = pltpu.VMEM((parts, rows * TIME, LANES), jnp.float32)
    late = pltpu.HBM((parts, rows * TIME, LANES), jnp.float32)
    late_spec = pl.BlockSpec((1, rows * TIME, LANES), lambda k, pos, order: (order[k], 0, 0))
    return pl.pallas_call(
        functools.partial(mixer_kernel, dims),
        out_shape=(shape, late),
        grid_spec=pltpu.PrefetchScalarGridSpec(
            num_scalar_prefetch=2,
            grid=(parts,),
            in_specs=[
                pl.BlockSpec((wins, streams, TIME, width), lambda k, pos, order: (0, 0, 0, order[k])),
                pl.BlockSpec((1,) + packed.shape[1:], lambda k, *_: (k, 0, 0)),
            ],
            out_specs=[pl.BlockSpec(memory_space=pltpu.VMEM), late_spec],
            scratch_shapes=[
                pltpu.VMEM((streams, rows * TIME, LANES), jnp.float32),
                pltpu.VMEM((rows * lead_rows, LANES), jnp.float32),
                pltpu.VMEM((rows * TAP_ROWS, LANES), jnp.float32),
                pltpu.VMEM((rows * TIME, LANES), jnp.float32),
                pltpu.VMEM((wins * BASE_ROWS, LANES), jnp.float32),
                pltpu.VMEM((TIME, rows, LANES), jnp.float32),
            ],
        ),
        compiler_params=pltpu.CompilerParams(vmem_limit_bytes=24 * 2**20),
        cost_estimate=pl.CostEstimate(flops=2 * 10**9, bytes_accessed=10 * 2**20, transcendentals=0),
        name="mixer",
    )(position, order, proj, packed)


def combine_kernel(gate_ref, part_hbm, carried_ref, out_ref, part_ref, sem):
    parts, rows, _ = gate_ref.shape
    wins, _, total = out_ref.shape
    blocks = rows // TIME // wins
    width = total // parts
    count = sem.shape[0]
    step = parts // count
    copies = []
    for c in range(count):
        span = pl.ds(c * step, step)
        copies.append(pltpu.make_async_copy(part_hbm.at[span], part_ref.at[span], sem.at[c]))
        copies[-1].start()
    for c in range(count):
        copies[c].wait()

        def body(i, carry):
            k = c * step + i
            for w in range(wins):
                for b in range(blocks):
                    at = slice((w * blocks + b) * TIME, (w * blocks + b + 1) * TIME)
                    lanes = pl.ds(pl.multiple_of(k * width + b * LANES, LANES), LANES)
                    filtered = part_ref[k, at, :] + carried_ref[k, at, :].astype(jnp.float32)
                    out_ref[w, :, lanes] = (gate_ref[k, at, :] * filtered).astype(jnp.bfloat16)
            return carry

        lax.fori_loop(0, step, body, 0)


def combine_of(gate, part, carried, wins):
    parts, rows, _ = gate.shape
    width = rows // TIME // wins * LANES
    return pl.pallas_call(
        combine_kernel,
        out_shape=jax.ShapeDtypeStruct((wins, TIME, parts * width), jnp.bfloat16),
        in_specs=[
            pl.BlockSpec(memory_space=pltpu.VMEM),
            pl.BlockSpec(memory_space=pltpu.HBM),
            pl.BlockSpec(memory_space=pltpu.VMEM),
        ],
        out_specs=pl.BlockSpec(memory_space=pltpu.VMEM),
        scratch_shapes=[pltpu.VMEM(part.shape, jnp.float32), pltpu.SemaphoreType.DMA((4,))],
        compiler_params=pltpu.CompilerParams(vmem_limit_bytes=24 * 2**20),
        name="combine",
    )(gate, pltpu.with_memory_space_constraint(part, pltpu.HBM), pltpu.with_memory_space_constraint(carried, pltpu.VMEM))


def rank_of(keys):
    count = keys.shape[-1]
    same = keys[..., :, None] == keys[..., None, :]
    earlier = jnp.arange(count)[None, :] < jnp.arange(count)[:, None]
    return jnp.sum((same & earlier).astype(jnp.int32), axis=-1)


def slots_of(mask, values, capacity):
    rank = jnp.cumsum(mask.astype(jnp.int32), axis=-1) - 1
    hit = mask[..., None, :] & (rank[..., None, :] == jnp.arange(capacity)[:, None])
    return jnp.sum(jnp.where(hit, values[..., None, :], 0), axis=-1)


def take_rows(array, index):
    return array.at[index].get(mode="promise_in_bounds")


def local(
    projected,
    cache_history,
    cache_inputs,
    feature_taps,
    filters,
    skip_weight,
    base_inputs,
    window_owner,
    window_slot,
    variant_position,
    allele,
):
    var_count, tp_count = lax.axis_size("var"), lax.axis_size("tp")
    me, part = lax.axis_index("var"), lax.axis_index("tp")
    windows, own = variant_position.shape[0], projected.shape[0]
    loci, _, width = cache_history.shape
    group_size = width // filters.shape[1]
    taps, streams = feature_taps.shape[:2]
    lead_len = cache_inputs.shape[1]
    filters_t = filters.T

    owners = window_owner.reshape(var_count, windows)
    slots = window_slot.reshape(var_count, windows)
    pick = slots_of(owners == me, slots, CAPACITY).reshape(-1)
    own_owner = lax.dynamic_index_in_dim(owners, me, 0, keepdims=False)
    own_row = own_owner * CAPACITY + rank_of(own_owner)

    def exchange(rows):
        got = lax.all_to_all(rows.reshape(var_count, -1, LANES), "var", split_axis=0, concat_axis=0, tiled=True)
        return got.reshape(rows.shape)

    lead = exchange(lead_of(me, window_owner, window_slot, cache_inputs, windows))
    carried = take_rows(owner_of(cache_history, filters_t, group_size), pick)
    params = params_of(feature_taps.transpose(1, 0, 2), skip_weight[None], filters_t)
    carried, lead, params = lax.optimization_barrier((carried, lead, params))
    carried = exchange(carried)

    half = tp_count // 2
    line, core = part // 2, part % 2
    steps = jnp.arange(half)
    targets = (line + steps) % half * 2
    near, far = pack_of(
        own,
        own_row,
        allele,
        jnp.concatenate([targets + core, targets + 1 - core]),
        lead,
        base_inputs.transpose(1, 0, 2),
        params,
    )
    other = lax.ppermute(far, "tp", [(k, k ^ 1) for k in range(tp_count)])
    both = [jnp.stack([near[step], other[step]]) for step in range(half)]
    for step in sorted(range(1, half), key=lambda step: -min(step, half - step)):
        both[step] = lax.ppermute(both[step], "tp", [(k, (k + 2 * step) % tp_count) for k in range(tp_count)])
    packed = jnp.concatenate(both, axis=0)
    sources = (line - steps) % half * 2
    order = jnp.stack([sources + core, sources + 1 - core], axis=1).reshape(-1)

    carried, _ = lax.optimization_barrier((carried, packed))
    carried = take_rows(carried, own_row).reshape(tp_count, -1, LANES)
    carried = lax.all_to_all(carried, "tp", split_axis=0, concat_axis=0, tiled=True)

    position = lax.dynamic_slice(variant_position, (part * own,), (own,))
    gate, partial = mixer_of(
        (taps, lead_len, filters_t.shape[0]), position, order, projected.transpose(0, 2, 1, 3), packed
    )
    return combine_of(gate, partial, carried, own)


def solution(mesh):
    return jax.shard_map(
        local,
        mesh=mesh,
        in_specs=(
            P(("var", "tp"), None, None, None),
            P("var", None, "tp"),
            P("var", None, None, "tp"),
            P(None, None, "tp"),
            P(None, "tp"),
            P("tp"),
            P(None, None, "tp"),
            P(),
            P(),
            P("var"),
            P("var"),
        ),
        out_specs=P(("var", "tp"), None, None),
        check_vma=False,
    )
```

```python
import functools
import jax
import jax.numpy as jnp
from jax import lax
from jax.experimental import pallas as pl
from jax.experimental.pallas import tpu as pltpu
from jax.sharding import PartitionSpec as P

LANES = 128
TAP_ROWS = 22
BASE_ROWS = 16
BASE_USED = 12
CAPACITY = 2
TIME = 32


def lead_kernel(windows, me_ref, owner_ref, slot_ref, inputs_ref, send_ref, rows_scr):
    loci, lead_len, streams, width = inputs_ref.shape
    blocks = width // LANES
    f32 = jnp.float32
    for n in range(loci):
        for r in range(lead_len):
            for b in range(blocks):
                at = ((n * blocks + b) * lead_len + r) * streams
                piece = inputs_ref[n, r, :, b * LANES : (b + 1) * LANES]
                rows_scr[at : at + streams, :] = piece.astype(f32)
    lanes = owner_ref.shape[1]
    row = lax.broadcasted_iota(jnp.int32, (lanes, lanes), 0)
    col = lax.broadcasted_iota(jnp.int32, (lanes, lanes), 1)
    before = ((row // windows == col // windows) & (row < col)).astype(jnp.bfloat16)
    gather = (row // windows == col).astype(jnp.bfloat16)
    mine = owner_ref[...] == me_ref[0]
    rank = jnp.dot(mine.astype(f32).astype(jnp.bfloat16), before, preferred_element_type=f32)
    slot = slot_ref[...].astype(f32)
    span = blocks * lead_len * streams
    segments = lanes // windows
    picks = []
    for r in range(CAPACITY):
        value = jnp.where(mine & (rank == r), slot, 0.0).astype(jnp.bfloat16)
        picks.append(jnp.dot(value, gather, preferred_element_type=f32))
    for i in range(send_ref.shape[0]):
        target, r = i // CAPACITY, i % CAPACITY
        pick = picks[r][target // segments : target // segments + 1, target % segments : target % segments + 1]
        pick = jnp.broadcast_to(pick, (span, LANES))
        found = rows_scr[:span, :]
        for n in range(1, loci):
            found = jnp.where(pick == n, rows_scr[n * span : (n + 1) * span, :], found)
        send_ref[i] = found.astype(jnp.bfloat16)


def lead_of(me, owners, slots, inputs, windows):
    loci, lead_len, streams, width = inputs.shape
    rows = width // LANES * lead_len * streams
    targets = slots.shape[0] // windows
    lanes = min(LANES, slots.shape[0])
    return pl.pallas_call(
        functools.partial(lead_kernel, windows),
        out_shape=jax.ShapeDtypeStruct((targets * CAPACITY, rows, LANES), jnp.bfloat16),
        in_specs=[pl.BlockSpec(memory_space=pltpu.SMEM)] + [pl.BlockSpec(memory_space=pltpu.VMEM)] * 3,
        out_specs=pl.BlockSpec(memory_space=pltpu.VMEM),
        scratch_shapes=[pltpu.VMEM((loci * rows, LANES), jnp.float32)],
        name="lead",
    )(me.reshape(1), owners.reshape(-1, lanes), slots.reshape(-1, lanes), inputs)


def owner_kernel(group_size, history_ref, filters_ref, carried_ref, line_scr):
    loci, history_len, width = history_ref.shape
    tap_count = filters_ref.shape[1]
    blocks = width // LANES
    per_block = LANES // group_size
    f32 = jnp.float32
    row = lax.broadcasted_iota(jnp.int32, (tap_count, tap_count), 0)
    col = lax.broadcasted_iota(jnp.int32, (tap_count, tap_count), 1)
    flip = (row + col == tap_count - 1).astype(jnp.bfloat16)
    line_scr[...] = jnp.dot(filters_ref[...], flip, preferred_element_type=f32)
    t_row = lax.broadcasted_iota(jnp.int32, (TIME, tap_count), 0)
    s_col = lax.broadcasted_iota(jnp.int32, (TIME, tap_count), 1)
    valid = (s_col >= t_row) & (s_col < history_len)
    lane = lax.broadcasted_iota(jnp.int32, (TIME, LANES), 1) // group_size
    for b in range(blocks):
        tables = []
        for g in range(per_block):
            index = b * per_block + g
            line = jnp.broadcast_to(line_scr[index : index + 1, :], (TIME, tap_count))
            turned = pltpu.roll(line, 0, 1, stride=1, stride_axis=0)
            tables.append(jnp.where(valid, turned, 0.0))
        table = jnp.concatenate(tables, axis=0).astype(jnp.bfloat16)[:, :history_len]
        for n in range(loci):
            past = history_ref[n, :, b * LANES : (b + 1) * LANES]
            full = jnp.dot(table, past, preferred_element_type=f32)
            total = jnp.zeros((TIME, LANES), f32)
            for g in range(per_block):
                total = jnp.where(lane == g, full[g * TIME : (g + 1) * TIME], total)
            carried_ref[n, b * TIME : (b + 1) * TIME, :] = total.astype(jnp.bfloat16)


def owner_of(history, filters_t, group_size):
    loci, _, width = history.shape
    return pl.pallas_call(
        functools.partial(owner_kernel, group_size),
        out_shape=jax.ShapeDtypeStruct((loci, width // LANES * TIME, LANES), jnp.bfloat16),
        in_specs=[pl.BlockSpec(memory_space=pltpu.VMEM)] * 2,
        out_specs=pl.BlockSpec(memory_space=pltpu.VMEM),
        scratch_shapes=[pltpu.VMEM(filters_t.shape, jnp.float32)],
        name="owner",
    )(history, filters_t)


def params_kernel(taps_ref, skip_ref, filters_ref, out_ref, par_scr, filt_scr):
    streams, taps, width = taps_ref.shape
    f32 = jnp.float32
    par_scr[...] = jnp.zeros_like(par_scr)
    for b in range(width // LANES):
        lanes = slice(b * LANES, (b + 1) * LANES)
        for s in range(streams):
            at = b * TAP_ROWS + s * taps
            par_scr[at : at + taps, :] = taps_ref[s, :, lanes].astype(f32)
        at = b * TAP_ROWS + streams * taps
        par_scr[at : at + 1, :] = skip_ref[:, lanes].astype(f32)
    rows = par_scr.shape[0]
    out_ref[:rows, :] = par_scr[...].astype(jnp.bfloat16)
    filt_scr[...] = filters_ref[...].astype(f32)
    share = LANES // TIME
    lines = filters_ref.shape[0] // share
    lane = lax.broadcasted_iota(jnp.int32, (lines, LANES), 1) // TIME
    packed = jnp.zeros((lines, LANES), f32)
    for m in range(share):
        line = filt_scr[pl.ds(m, lines, stride=share), :]
        line = pltpu.roll(line, m * TIME, 1) if m else line
        packed = jnp.where(lane == m, line, packed)
    out_ref[rows:, :] = packed.astype(jnp.bfloat16)


def params_of(taps, skip, filters_t):
    rows = taps.shape[2] // LANES * TAP_ROWS
    return pl.pallas_call(
        params_kernel,
        out_shape=jax.ShapeDtypeStruct((rows + filters_t.shape[0] * TIME // LANES, LANES), jnp.bfloat16),
        in_specs=[pl.BlockSpec(memory_space=pltpu.VMEM)] * 3,
        out_specs=pl.BlockSpec(memory_space=pltpu.VMEM),
        scratch_shapes=[pltpu.VMEM((rows, LANES), jnp.float32), pltpu.VMEM(filters_t.shape, jnp.float32)],
        name="params",
    )(taps, skip, filters_t)


def pack_kernel(own, row_ref, allele_ref, order_ref, got_ref, base_ref, params_ref, near_ref, far_ref, base_scr, pair_scr):
    half = near_ref.shape[0]
    lead_rows = got_ref.shape[1]
    streams, bases, width = base_ref.shape
    base_scr[...] = jnp.zeros_like(base_scr)
    for b in range(width // LANES):
        for s in range(streams):
            for letter in range(bases):
                at = letter * BASE_ROWS + b * streams + s
                piece = base_ref[s, letter : letter + 1, b * LANES : (b + 1) * LANES]
                base_scr[at : at + 1, :] = piece.astype(jnp.float32)
    first = own * lead_rows
    for half_index, out_ref in enumerate((near_ref, far_ref)):

        def fill(i, carry):
            k = order_ref[half_index * half + i]
            out_ref[i, first + own * BASE_USED :, :] = params_ref[...]
            for w in range(own):
                out_ref[i, w * lead_rows : (w + 1) * lead_rows, :] = got_ref[row_ref[k * own + w]]
                source = pl.multiple_of(allele_ref[k * own + w] * BASE_ROWS, BASE_ROWS)
                piece = base_scr[pl.ds(source, BASE_ROWS), :]
                pair_scr[w * BASE_USED : (w + 1) * BASE_USED, :] = piece[:BASE_USED]
            out_ref[i, first : first + own * BASE_USED, :] = pair_scr[...].astype(jnp.bfloat16)
            return carry

        lax.fori_loop(0, half, fill, 0)


def pack_of(own, row, allele, order, got, base, params):
    rows = own * (got.shape[1] + BASE_USED) + params.shape[0]
    half = jax.ShapeDtypeStruct((order.shape[0] // 2, rows, LANES), jnp.bfloat16)
    return pl.pallas_call(
        functools.partial(pack_kernel, own),
        out_shape=(half, half),
        in_specs=[pl.BlockSpec(memory_space=pltpu.SMEM)] * 3 + [pl.BlockSpec(memory_space=pltpu.VMEM)] * 3,
        out_specs=[pl.BlockSpec(memory_space=pltpu.VMEM)] * 2,
        scratch_shapes=[
            pltpu.VMEM((base.shape[1] * BASE_ROWS, LANES), jnp.float32),
            pltpu.VMEM((own * BASE_USED, LANES), jnp.float32),
        ],
        compiler_params=pltpu.CompilerParams(vmem_limit_bytes=24 * 2**20),
        name="pack",
    )(row, allele, order, pltpu.with_memory_space_constraint(got, pltpu.VMEM), base, params)


def mixer_kernel(dims, pos_ref, order_ref, proj_ref, pack_ref, gate_ref, part_ref,
                 x_scr, l_scr, p_scr, f_scr, b_scr, m_scr):
    taps, lead_len, groups = dims
    place = order_ref[pl.program_id(0)]
    wins, streams, _, width = proj_ref.shape
    blocks = width // LANES
    rows = wins * blocks
    lead_rows = lead_len * streams
    f32 = jnp.float32
    span = blocks * lead_rows
    first = wins * span
    par_rows = blocks * TAP_ROWS
    shared = first + wins * BASE_USED
    share = LANES // TIME
    lines = groups // share
    filt = pack_ref[0, shared + par_rows : shared + par_rows + lines, :]
    line = lax.broadcasted_iota(jnp.int32, (lines, width), 0) * share
    group = lax.broadcasted_iota(jnp.int32, (lines, width), 1) // (width // groups)
    wide = jnp.zeros((TIME, width), f32)
    for m in range(share):
        spread = (line + m == group).astype(jnp.bfloat16)
        part = filt[:, m * TIME : (m + 1) * TIME]
        wide += lax.dot_general(part, spread, (((0,), (0,)), ((), ())), preferred_element_type=f32)
    b_scr[...] = pack_ref[0, first:shared, :].astype(f32)
    for w in range(wins):
        l_scr[w * span : (w + 1) * span, :] = pack_ref[0, w * span : (w + 1) * span, :].astype(f32)
        p_scr[w * par_rows : (w + 1) * par_rows, :] = pack_ref[0, shared : shared + par_rows, :].astype(f32)
        for b in range(blocks):
            q = w * blocks + b
            lanes = slice(b * LANES, (b + 1) * LANES)
            f_scr[q * TIME : (q + 1) * TIME, :] = wide[:, lanes]
            for s in range(streams):
                x_scr[s, q * TIME : (q + 1) * TIME, :] = proj_ref[w, s, :, lanes].astype(f32)
    for w in range(wins):
        for s in range(streams):
            for b in range(blocks):
                q = w * blocks + b
                source = w * BASE_USED + b * streams + s
                x_scr[s, pl.ds(q * TIME + pos_ref[w], 1), :] = b_scr[source : source + 1, :]

    def param(r):
        return p_scr[pl.ds(r, rows, stride=TAP_ROWS), :]

    def entry(s, r):
        if r < lead_len:
            return l_scr[pl.ds(r * streams + s, rows, stride=lead_rows), :]
        return x_scr[s, pl.ds(r - lead_len, rows, stride=TIME), :]

    def featured(s):
        weight = [param(s * taps + j) for j in range(taps)]
        window = [entry(s, r) for r in range(taps - 1)]
        for t in range(TIME):
            window.append(entry(s, t + taps - 1))
            total = weight[0] * window[taps - 1]
            for j in range(1, taps):
                total = total + weight[j] * window[taps - 1 - j]
            window.pop(0)
            yield total

    for t, (one, two) in enumerate(zip(featured(1), featured(2))):
        m_scr[t] = (one * two).astype(jnp.bfloat16).astype(f32)
    skip = param(streams * taps)
    for t, gate in enumerate(featured(0)):
        gate_ref[place, pl.ds(t, rows, stride=TIME), :] = gate
    step = 8
    for start in range(0, TIME, step):
        total = [None] * step
        for j in range(start + step):
            tap = f_scr[pl.ds(j, rows, stride=TIME), :]
            for i in range(step):
                at = start + i - j
                if at >= 0:
                    term = tap * m_scr[at]
                    total[i] = term if total[i] is None else total[i] + term
        for i in range(step):
            t = start + i
            part_ref[0, pl.ds(t, rows, stride=TIME), :] = total[i] + skip * m_scr[t]


def mixer_of(dims, position, order, proj, packed):
    wins, streams, _, total = proj.shape
    parts = packed.shape[0]
    width = total // parts
    blocks = width // LANES
    rows = wins * blocks
    lead_rows = dims[1] * streams
    shape = pltpu.VMEM((parts, rows * TIME, LANES), jnp.float32)
    late = pltpu.HBM((parts, rows * TIME, LANES), jnp.float32)
    late_spec = pl.BlockSpec((1, rows * TIME, LANES), lambda k, pos, order: (order[k], 0, 0))
    return pl.pallas_call(
        functools.partial(mixer_kernel, dims),
        out_shape=(shape, late),
        grid_spec=pltpu.PrefetchScalarGridSpec(
            num_scalar_prefetch=2,
            grid=(parts,),
            in_specs=[
                pl.BlockSpec((wins, streams, TIME, width), lambda k, pos, order: (0, 0, 0, order[k])),
                pl.BlockSpec((1,) + packed.shape[1:], lambda k, *_: (k, 0, 0)),
            ],
            out_specs=[pl.BlockSpec(memory_space=pltpu.VMEM), late_spec],
            scratch_shapes=[
                pltpu.VMEM((streams, rows * TIME, LANES), jnp.float32),
                pltpu.VMEM((rows * lead_rows, LANES), jnp.float32),
                pltpu.VMEM((rows * TAP_ROWS, LANES), jnp.float32),
                pltpu.VMEM((rows * TIME, LANES), jnp.float32),
                pltpu.VMEM((wins * BASE_USED, LANES), jnp.float32),
                pltpu.VMEM((TIME, rows, LANES), jnp.float32),
            ],
        ),
        compiler_params=pltpu.CompilerParams(vmem_limit_bytes=24 * 2**20),
        cost_estimate=pl.CostEstimate(flops=2 * 10**9, bytes_accessed=10 * 2**20, transcendentals=0),
        name="mixer",
    )(position, order, proj, packed)


def combine_kernel(gate_ref, part_hbm, carried_ref, out_ref, part_ref, sem):
    parts, rows, _ = gate_ref.shape
    wins, _, total = out_ref.shape
    blocks = rows // TIME // wins
    width = total // parts
    count = sem.shape[0]
    step = parts // count
    copies = []
    for c in range(count):
        span = pl.ds(c * step, step)
        copies.append(pltpu.make_async_copy(part_hbm.at[span], part_ref.at[span], sem.at[c]))
        copies[-1].start()
    for c in range(count):
        copies[c].wait()

        def body(i, carry):
            k = c * step + i
            for w in range(wins):
                for b in range(blocks):
                    at = slice((w * blocks + b) * TIME, (w * blocks + b + 1) * TIME)
                    lanes = pl.ds(pl.multiple_of(k * width + b * LANES, LANES), LANES)
                    filtered = part_ref[k, at, :] + carried_ref[k, at, :].astype(jnp.float32)
                    out_ref[w, :, lanes] = (gate_ref[k, at, :] * filtered).astype(jnp.bfloat16)
            return carry

        lax.fori_loop(0, step, body, 0)


def combine_of(gate, part, carried, wins):
    parts, rows, _ = gate.shape
    width = rows // TIME // wins * LANES
    return pl.pallas_call(
        combine_kernel,
        out_shape=jax.ShapeDtypeStruct((wins, TIME, parts * width), jnp.bfloat16),
        in_specs=[
            pl.BlockSpec(memory_space=pltpu.VMEM),
            pl.BlockSpec(memory_space=pltpu.HBM),
            pl.BlockSpec(memory_space=pltpu.VMEM),
        ],
        out_specs=pl.BlockSpec(memory_space=pltpu.VMEM),
        scratch_shapes=[pltpu.VMEM(part.shape, jnp.float32), pltpu.SemaphoreType.DMA((4,))],
        compiler_params=pltpu.CompilerParams(vmem_limit_bytes=24 * 2**20),
        name="combine",
    )(gate, pltpu.with_memory_space_constraint(part, pltpu.HBM), pltpu.with_memory_space_constraint(carried, pltpu.VMEM))


def rank_of(keys):
    count = keys.shape[-1]
    same = keys[..., :, None] == keys[..., None, :]
    earlier = jnp.arange(count)[None, :] < jnp.arange(count)[:, None]
    return jnp.sum((same & earlier).astype(jnp.int32), axis=-1)


def slots_of(mask, values, capacity):
    rank = jnp.cumsum(mask.astype(jnp.int32), axis=-1) - 1
    hit = mask[..., None, :] & (rank[..., None, :] == jnp.arange(capacity)[:, None])
    return jnp.sum(jnp.where(hit, values[..., None, :], 0), axis=-1)


def take_rows(array, index):
    return array.at[index].get(mode="promise_in_bounds")


def local(
    projected,
    cache_history,
    cache_inputs,
    feature_taps,
    filters,
    skip_weight,
    base_inputs,
    window_owner,
    window_slot,
    variant_position,
    allele,
):
    var_count, tp_count = lax.axis_size("var"), lax.axis_size("tp")
    me, part = lax.axis_index("var"), lax.axis_index("tp")
    windows, own = variant_position.shape[0], projected.shape[0]
    loci, _, width = cache_history.shape
    group_size = width // filters.shape[1]
    taps, streams = feature_taps.shape[:2]
    lead_len = cache_inputs.shape[1]
    filters_t = filters.T

    owners = window_owner.reshape(var_count, windows)
    slots = window_slot.reshape(var_count, windows)
    pick = slots_of(owners == me, slots, CAPACITY).reshape(-1)
    own_owner = lax.dynamic_index_in_dim(owners, me, 0, keepdims=False)
    own_row = own_owner * CAPACITY + rank_of(own_owner)

    def exchange(rows):
        got = lax.all_to_all(rows.reshape(var_count, -1, LANES), "var", split_axis=0, concat_axis=0, tiled=True)
        return got.reshape(rows.shape)

    lead = exchange(lead_of(me, window_owner, window_slot, cache_inputs, windows))
    carried = take_rows(owner_of(cache_history, filters_t, group_size), pick)
    params = params_of(feature_taps.transpose(1, 0, 2), skip_weight[None], filters_t)
    carried, lead, params = lax.optimization_barrier((carried, lead, params))
    carried = exchange(carried)

    half = tp_count // 2
    line, core = part // 2, part % 2
    steps = jnp.arange(half)
    targets = (line + steps) % half * 2
    near, far = pack_of(
        own,
        own_row,
        allele,
        jnp.concatenate([targets + core, targets + 1 - core]),
        lead,
        base_inputs.transpose(1, 0, 2),
        params,
    )
    other = lax.ppermute(far, "tp", [(k, k ^ 1) for k in range(tp_count)])
    both = [jnp.stack([near[step], other[step]]) for step in range(half)]
    for step in sorted(range(1, half), key=lambda step: -min(step, half - step)):
        both[step] = lax.ppermute(both[step], "tp", [(k, (k + 2 * step) % tp_count) for k in range(tp_count)])
    packed = jnp.concatenate(both, axis=0)
    sources = (line - steps) % half * 2
    order = jnp.stack([sources + core, sources + 1 - core], axis=1).reshape(-1)

    carried, _ = lax.optimization_barrier((carried, packed))
    carried = take_rows(carried, own_row).reshape(tp_count, -1, LANES)
    carried = lax.all_to_all(carried, "tp", split_axis=0, concat_axis=0, tiled=True)

    position = lax.dynamic_slice(variant_position, (part * own,), (own,))
    gate, partial = mixer_of(
        (taps, lead_len, filters_t.shape[0]), position, order, projected.transpose(0, 2, 1, 3), packed
    )
    return combine_of(gate, partial, carried, own)


def solution(mesh):
    return jax.shard_map(
        local,
        mesh=mesh,
        in_specs=(
            P(("var", "tp"), None, None, None),
            P("var", None, "tp"),
            P("var", None, None, "tp"),
            P(None, None, "tp"),
            P(None, "tp"),
            P("tp"),
            P(None, None, "tp"),
            P(),
            P(),
            P("var"),
            P("var"),
        ),
        out_specs=P(("var", "tp"), None, None),
        check_vma=False,
    )
```
